512 devices in a mesh: dp: 16 (over y, core), expert: 32 (over z, x).
Axes of the slice: x: 4, y: 8, z: 8, core: 2. Of those that a mesh axis runs over, the one named last changes fastest.
Arguments:
- queries: bfloat16 [16, 4096, 2048], P('dp', 'expert'), may hold values from -5.5 to 5.5
- keys: bfloat16 [16, 4096, 2048], P('dp', 'expert'), may hold values from -5.5 to 5.5
- values: bfloat16 [16, 4096, 2048], P('dp', 'expert'), may hold values from -6 to 6
- doc_ids: int32 [16, 4096], P('dp', 'expert'), may hold values from 0 to 7, never falling along the last dimension, each value on 1 to 1024 neighbouring positions
- expert_index: int32 [16, 4096, 2], P('dp', 'expert'), may hold values from 0 to 31, all different within a row; in each aligned block of 128 rows (0 to 127, 128 to 255, ..., all dimensions but the last counted through in order) at most 12 rows name the same one
- gates: float32 [16, 4096, 2], P('dp', 'expert'), may hold values from 0.1 to 1
- capacity: int32 [32], replicated, may hold values from 6 to 12, as said below
- norm_gain: float32 [2048], replicated, may hold values from 0.1 to 1.9
- gate_weight: bfloat16 [32, 2048, 1024], P('expert', 'dp'), may hold values from -0.125 to 0.125
- up_weight: bfloat16 [32, 2048, 1024], P('expert', 'dp'), may hold values from -0.125 to 0.125
- down_weight: bfloat16 [32, 1024, 2048], P('expert', 'dp'), may hold values from -0.1875 to 0.1875
Outputs:
- mixed: bfloat16 [16, 4096, 2048], P('dp', 'expert')
The draws below stay inside these ranges and needn't reach their ends.
Inputs may be any that keep to these rules, and one draw needn't show every extreme that they name: `doc_ids`: never falls along a window; each protein has 1 to 1024 residues, one exactly 1024; every number of proteins below 8 appears. `expert_index`: the two experts of a residue differ; within the 128 residues of one device (aligned blocks of a window) no expert is named by more than 12 residues, a bound that some block reaches. Some expert has capacity exactly 12.
All inputs are finite; a program needn't handle non-finite values.
Results may differ from the reference program's by a relative error of at most 0.017.
Values may be sent and summed in bfloat16 or wider, within the bound.
A program may use at most 64 MiB of HBM per device.

```python
import math
import jax
import jax.numpy as jnp
import numpy as np
from jax import lax

HEAD_DIM = 128
D = 2048
FF = 1024
TOP = 2
WINDOW = 512
TOK_DEV = 128
EXPERTS = 32
WINDOWS = 16
LENGTH = 4096
MOST = 12
DOCS = 8
DOC_MOST = 1024


def base_field(key):
    return jnp.clip(jax.random.normal(key, (WINDOWS, LENGTH, D), jnp.float32), -4.0, 4.0)


def draw_queries(key, part):
    drawn = base_field(jax.random.fold_in(key, 31))
    return drawn.astype(jnp.bfloat16)


def draw_keys(key, part):
    drawn = base_field(jax.random.fold_in(key, 32))
    return drawn.astype(jnp.bfloat16)


def draw_capacity(key, part):
    limits = jax.random.randint(jax.random.fold_in(key, 21), (EXPERTS,), (MOST + 1) // 2, MOST + 1)
    fullest = jax.random.randint(jax.random.fold_in(key, 22), (), 0, EXPERTS)
    return jnp.where(jnp.arange(EXPERTS, dtype=jnp.int32) == fullest, MOST, limits).astype(jnp.int32)


def steps_of(rng, shape, pieces, smallest, top_value):
    gain = 1.0
    for axis_at, parts in pieces:
        draws = jax.random.uniform(jax.random.fold_in(jax.random.fold_in(rng, 6), axis_at), (parts,), jnp.float32, smallest / len(pieces), top_value / len(pieces))
        gain = gain * jnp.repeat(jnp.exp(draws), shape[axis_at] // parts).reshape((-1,) + (1,) * (len(shape) - 1 - axis_at))
    return gain


def length_profile(number_of, total, bound, slope):
    portions = [(1 << 20) // math.isqrt(standing ** slope) + 1 for standing in range(2, number_of + 1)]
    rest, given = total - bound - (number_of - 1), [1] * (number_of - 1)
    while rest > 0:
        candidates = [i for i in range(number_of - 1) if given[i] < bound]
        mass, remaining = sum([portions[i] for i in candidates]), rest
        for i in candidates:
            extra = min(bound - given[i], max(1, remaining * portions[i] // mass), rest)
            given[i] = given[i] + extra
            rest = rest - extra
    return np.array([bound] + given)


def uneven(key, number_of, total, limit, slope):
    if number_of == 2:
        one = jax.random.randint(key, (), max(1, total - limit), min(limit, total - 1) + 1)
        return jnp.stack([one, total - one])
    lengths = jnp.asarray(length_profile(number_of, total, limit, slope), jnp.int32)
    twos = (number_of - 1) // 2
    source_of, sink = lengths[1:1 + 2 * twos:2], lengths[2:2 + 2 * twos:2]
    slack = jnp.minimum(source_of - 1, limit - sink)
    moved = jax.random.randint(jax.random.fold_in(key, 1), (twos,), 0, 1 << 20) % (slack + 1)
    lengths = lengths.at[1:1 + 2 * twos:2].set(source_of - moved).at[2:2 + 2 * twos:2].set(sink + moved)
    return lengths[jax.random.permutation(jax.random.fold_in(key, 2), number_of)]


def routed_block(stream_key, own, number, rows, amount, top, bound, skew):
    order = jax.random.permutation(stream_key, amount)
    heavy_load, ordinary = shares(amount, rows * top, bound, skew, True), shares(amount, rows * top, bound, skew, False)
    places = jnp.arange(amount)

    def named(tallies, offset_by):
        used = int((tallies > 0).sum())
        fixed = max(1, used // 4)
        passed = fixed + (places - fixed + offset_by * (used - fixed)) % max(1, amount - fixed)
        return jnp.zeros((amount,), jnp.int32).at[order[jnp.where(places < fixed, places, passed)]].set(jnp.asarray(tallies, jnp.int32))

    tallies = jnp.where(number % 4 == 0, named(heavy_load, number // 4), named(ordinary, number - number // 4 - 1))
    mixed = jax.random.permutation(jax.random.fold_in(own, 3), amount)
    donor, sink = mixed[0:amount // 2 * 2:2], mixed[1:amount // 2 * 2:2]
    margin = jnp.minimum(tallies[donor] - 1, bound - tallies[sink]) // 2
    margin = jnp.where((donor == order[0]) | (sink == order[0]) | (tallies[sink] == 0), 0, jnp.maximum(margin, 0))
    passed = jax.random.randint(jax.random.fold_in(own, 4), (amount // 2,), 0, 1 << 20) % (margin + 1)
    tallies = tallies.at[donor].add(-passed).at[sink].add(passed)
    members = jnp.searchsorted(jnp.cumsum(tallies), jnp.arange(rows * top), side="right").astype(jnp.int32)
    table = members.reshape(top, rows).T
    table = table[jax.random.permutation(jax.random.fold_in(own, 1), rows)]
    offset_by = jax.random.randint(jax.random.fold_in(own, 2), (rows, 1), 0, top)
    return jnp.take_along_axis(table, (jnp.arange(top)[None, :] + offset_by) % top, axis=1)


def shares(count, total, limit, lean, full):
    portions = [(1 << 20) // math.isqrt(standing ** lean) + 1 for standing in range(1, count + 1)]
    largest = limit if full else min(limit, max(-(-total // count), total * portions[0] // sum(portions)))
    least = 1 if total - largest >= count - 1 else 0
    holding, rest = [largest] + [least] * (count - 1), total - largest - least * (count - 1)
    while rest > 0:
        movable = [i for i in range(1, count) if holding[i] < largest] or [i for i in range(1, count) if holding[i] < limit]
        pool, left = sum([portions[i] for i in movable]), rest
        for i in movable:
            extra = min(limit - holding[i], max(1, left * portions[i] // pool), rest)
            holding[i] = holding[i] + extra
            rest = rest - extra
    return np.array(holding)


def scatter_about(stream_key, dims, spread, bound, split=(), held_as=jnp.bfloat16):
    values = jax.random.normal(stream_key, dims, jnp.float32) * spread
    if len(split) > 0:
        values = steps_of(stream_key, dims, split, -0.22, 0.18) * values
    return jnp.clip(values, min=-bound, max=bound).astype(held_as)


def setup_inputs(seed: int = 0) -> dict:
    splits = jax.random.split(jax.random.key(seed), 12)
    queries = draw_queries(jax.random.fold_in(splits[11], 71), 0)
    keys = draw_keys(jax.random.fold_in(splits[11], 71), 0)
    values = scatter_about(splits[2], (WINDOWS, LENGTH, D), 1.0, 6.0, ((0, 16), (1, 32)))
    doc_ids = jax.vmap(lambda own: jnp.searchsorted(jnp.cumsum(uneven(own, DOCS, LENGTH, DOC_MOST, 1)), jnp.arange(LENGTH), side="right"))(jax.random.split(splits[3], WINDOWS)).reshape((WINDOWS, LENGTH)).astype(jnp.int32)
    expert_index_keys = jax.random.split(jax.random.fold_in(splits[4], 1), WINDOWS * LENGTH // TOK_DEV)
    expert_index_turns = jax.random.permutation(jax.random.fold_in(splits[4], 3), WINDOWS * LENGTH // TOK_DEV)
    expert_index = jax.vmap(lambda own, number: routed_block(jax.random.fold_in(splits[4], 2), own, number, TOK_DEV, EXPERTS, TOP, MOST, 2))(expert_index_keys, expert_index_turns).reshape((WINDOWS, LENGTH, TOP))
    gates = jnp.clip(jnp.exp(math.log(1.0) - 2.3025851 * jax.random.uniform(splits[5], (WINDOWS, LENGTH, TOP), jnp.float32) ** steps_of(splits[5], (WINDOWS, LENGTH, TOP), ((0, 16), (1, 32)), -0.2, 0.2)), 0.1, 1.0)
    capacity = draw_capacity(jax.random.fold_in(splits[11], 71), 0)
    norm_gain = jnp.clip(1.0 + 0.18 * jax.random.normal(splits[7], (D,), jnp.float32), 0.1, 1.9)
    gate_weight = scatter_about(splits[8], (EXPERTS, D, FF), D ** -0.5, 0.125, ((0, 32), (1, 16)))
    up_weight = scatter_about(splits[9], (EXPERTS, D, FF), D ** -0.5, 0.125, ((0, 32), (1, 16)))
    down_weight = scatter_about(splits[10], (EXPERTS, FF, D), FF ** -0.5, 0.1875, ((0, 32), (1, 16)))
    return dict(queries=queries, keys=keys, values=values, doc_ids=doc_ids, expert_index=expert_index, gates=gates, capacity=capacity, norm_gain=norm_gain, gate_weight=gate_weight, up_weight=up_weight, down_weight=down_weight)


def attend_window(queries, keys, values, doc_row):
    length = queries.shape[0]
    width = queries.shape[1]
    heads = width // HEAD_DIM
    q_block = min(512, length)
    keys_pad = jnp.pad(keys, ((WINDOW, 0), (0, 0)))
    values_pad = jnp.pad(values, ((WINDOW, 0), (0, 0)))
    docs_pad = jnp.pad(doc_row, (WINDOW, 0), constant_values=-1)

    def one_block(number):
        begin = number * q_block
        query_rows = lax.dynamic_slice_in_dim(queries, begin, q_block, 0).astype(jnp.float32).reshape(q_block, heads, HEAD_DIM)
        key_rows = lax.dynamic_slice_in_dim(keys_pad, begin, q_block + WINDOW, 0).astype(jnp.float32).reshape(q_block + WINDOW, heads, HEAD_DIM)
        value_rows = lax.dynamic_slice_in_dim(values_pad, begin, q_block + WINDOW, 0).astype(jnp.float32).reshape(q_block + WINDOW, heads, HEAD_DIM)
        query_docs = lax.dynamic_slice_in_dim(doc_row, begin, q_block, 0)
        key_docs = lax.dynamic_slice_in_dim(docs_pad, begin, q_block + WINDOW, 0)
        query_pos = begin + jnp.arange(q_block, dtype=jnp.int32)
        key_pos = begin - WINDOW + jnp.arange(q_block + WINDOW, dtype=jnp.int32)
        allowed = (key_pos[None, :] <= query_pos[:, None]) & (key_pos[None, :] > query_pos[:, None] - WINDOW) & (key_docs[None, :] == query_docs[:, None])
        scores = jnp.einsum('qhd,khd->hqk', query_rows, key_rows) * (1.0 / math.sqrt(HEAD_DIM))
        scores = jnp.where(allowed[None], scores, -1e+30)
        highest = lax.optimization_barrier(jnp.max(scores, axis=-1, keepdims=True))
        expo = jnp.exp(scores - highest)
        probs = (expo / lax.optimization_barrier(jnp.sum(expo, axis=-1, keepdims=True))).astype(jnp.bfloat16)
        result = jnp.einsum('hqk,khd->qhd', probs.astype(jnp.float32), value_rows)
        return result.reshape(q_block, width).astype(jnp.bfloat16)
    blocks = lax.map(one_block, jnp.arange(length // q_block, dtype=jnp.int32))
    return blocks.reshape(length, width)

def expert_block(rows, w_gate, w_up, w_down):
    gate = jnp.dot(rows, w_gate, preferred_element_type=jnp.float32)
    upward = jnp.dot(rows, w_up, preferred_element_type=jnp.float32)
    hidden = (jax.nn.silu(gate) * upward).astype(jnp.bfloat16)
    return jnp.dot(hidden, w_down, preferred_element_type=jnp.float32).astype(jnp.bfloat16)

def reference(queries, keys, values, doc_ids, expert_index, gates, capacity, norm_gain, gate_weight, up_weight, down_weight):
    attended = lax.map(lambda packed: attend_window(packed[0], packed[1], packed[2], packed[3]), (queries, keys, values, doc_ids))
    flat_att = attended.reshape(-1, D).astype(jnp.float32)
    normed = (flat_att * lax.rsqrt(lax.optimization_barrier(jnp.mean(flat_att * flat_att, axis=-1, keepdims=True)) + 1e-05) * norm_gain).astype(jnp.bfloat16)
    total_rows = flat_att.shape[0]
    blocks = total_rows // TOK_DEV
    chosen = expert_index.reshape(blocks, TOK_DEV * TOP)
    onehot = (chosen[..., None] == jnp.arange(EXPERTS, dtype=jnp.int32)).astype(jnp.int32)
    ranks = lax.optimization_barrier(jnp.sum(onehot * (jnp.cumsum(onehot, axis=1) - 1), axis=-1))
    limits = lax.optimization_barrier(jnp.sum(onehot * capacity, axis=-1))
    kept_flat = (ranks < limits).reshape(-1)
    chosen_flat = chosen.reshape(-1)
    ranks_flat = ranks.reshape(-1)
    assign_ids = jnp.arange(total_rows * TOP, dtype=jnp.int32)
    block_id = assign_ids // (TOK_DEV * TOP)
    slot = block_id * MOST + ranks_flat
    token = assign_ids // TOP
    span = blocks * MOST

    def run_expert(number):
        target = jnp.where((chosen_flat == number) & kept_flat, slot, span)
        slot_token = jnp.full((span,), -1, jnp.int32).at[target].set(token, mode='drop')
        rows = jnp.where((slot_token >= 0)[:, None], normed[jnp.maximum(slot_token, 0)], jnp.zeros((), jnp.bfloat16))
        return expert_block(rows, gate_weight[number], up_weight[number], down_weight[number])
    outputs = lax.map(run_expert, jnp.arange(EXPERTS, dtype=jnp.int32)).reshape(EXPERTS * span, D)
    where_from = jnp.where(kept_flat, chosen_flat * span + slot, 0)
    weight = jnp.where(kept_flat, gates.reshape(-1), 0.0).reshape(total_rows, TOP)
    picked = outputs[where_from].reshape(total_rows, TOP, D)
    combined = flat_att
    for which in range(TOP):
        combined = combined + picked[:, which].astype(jnp.float32) * weight[:, which:which + 1]
    return combined.astype(jnp.bfloat16).reshape(WINDOWS, LENGTH, D)
```

```python
import functools
import math

import jax
import jax.numpy as jnp
from jax import lax
from jax.experimental import pallas as pl
from jax.experimental.pallas import tpu as pltpu
from jax.sharding import PartitionSpec as P

HEAD_DIM = 128
TOP = 2
GROUP = 4
MOST = 12
CHUNKS = 2
MESH = pl.DeviceIdType.MESH
BF = jnp.bfloat16
F32 = jnp.float32


def layer_kernel(
    experts,
    dp,
    q_in,
    k_in,
    v_in,
    meta_in,
    cap_in,
    gain_in,
    wg_in,
    wu_in,
    wd_in,
    out,
    qbuf,
    kbuf,
    vbuf,
    metabuf,
    keyrow,
    keycol,
    docrow,
    pick,
    mix,
    att,
    sbuf,
    xbuf,
    hbuf,
    ybuf,
    rbuf,
    fbuf,
    wgf,
    wuf,
    wdf,
    q_sem,
    kv_sem,
    halo_sem,
    meta_sem,
    disp_sem,
    ret_sem,
    fin_sem,
    ring_sem,
    part_sem,
    own_sem,
    qkv_send,
    halo_send,
    meta_send,
    disp_send,
    ret_send,
    fin_send,
    w_send,
):
    rows, width = q_in.shape
    cols = width // GROUP
    chunk = cols // CHUNKS
    heads = chunk // HEAD_DIM
    span = GROUP * rows
    slots = GROUP * MOST
    planes = experts // GROUP
    ring = dp // 2
    hops = ring // 2

    me = lax.axis_index("expert")
    z, x = lax.div(me, GROUP), lax.rem(me, GROUP)
    d = lax.axis_index("dp")
    y, core = lax.div(d, 2), lax.rem(d, 2)
    z_next = lax.rem(z + 1, planes)

    def at(start, size, unit):
        return pl.ds(pl.multiple_of(start, unit), size)

    def send(src, dst, send_sem, recv_sem, where):
        pltpu.make_async_remote_copy(
            src_ref=src, dst_ref=dst, send_sem=send_sem, recv_sem=recv_sem, device_id=where, device_id_type=MESH
        ).start()

    def local(src, dst, sem):
        pltpu.make_async_copy(src, dst, sem).start()

    def wait(ref, sem):
        pltpu.make_async_copy(ref, ref, sem).wait()

    barrier = pltpu.get_barrier_semaphore()

    def greet(i, carry):
        pl.semaphore_signal(barrier, inc=1, device_id={"expert": lax.rem(me + i, experts)}, device_id_type=MESH)
        return carry

    lax.fori_loop(1, experts, greet, 0)
    up, down, partner = lax.rem(y + 1, ring) * 2 + core, lax.rem(y + ring - 1, ring) * 2 + core, y * 2 + 1 - core
    for other in (up, down, partner):
        pl.semaphore_signal(barrier, inc=1, device_id={"dp": other}, device_id_type=MESH)
    pl.semaphore_wait(barrier, experts + 2)

    for i in range(1, GROUP):
        there = z * GROUP + lax.rem(x + i, GROUP)
        send(meta_in, metabuf.at[GROUP + x], meta_send, meta_sem, {"expert": there})
    for i in range(GROUP):
        send(meta_in, metabuf.at[x], meta_send, meta_sem, {"expert": z_next * GROUP + i})

    for c in range(CHUNKS):
        here = pl.ds(c * chunk, chunk)
        for i in range(1, GROUP):
            peer = lax.rem(x + i, GROUP)
            theirs = at(peer * cols + c * chunk, chunk, HEAD_DIM)
            there = {"expert": z * GROUP + peer}
            send(k_in.at[:, theirs], kbuf.at[at(span + x * rows, rows, rows), here], qkv_send.at[1], kv_sem.at[c], there)
            send(v_in.at[:, theirs], vbuf.at[at(span + x * rows, rows, rows), here], qkv_send.at[2], kv_sem.at[c], there)
            send(q_in.at[:, theirs], qbuf.at[at(x * rows, rows, rows), here], qkv_send.at[0], q_sem.at[c], there)
        mine = at(x * cols + c * chunk, chunk, HEAD_DIM)
        local(k_in.at[:, mine], kbuf.at[at(span + x * rows, rows, rows), here], kv_sem.at[c])
        local(v_in.at[:, mine], vbuf.at[at(span + x * rows, rows, rows), here], kv_sem.at[c])
        local(q_in.at[:, mine], qbuf.at[at(x * rows, rows, rows), here], q_sem.at[c])

    weights = ((wg_in, wgf), (wu_in, wuf), (wd_in, wdf))

    def block_of(piece, number, half):
        size = weights[piece][0].shape[0]
        base = (number * 2 + core) * size
        if half is None:
            return at(base, size, size)
        return at(base + half * (size // 2), size // 2, size // 2)

    def half_at(step, way):
        return way if step == hops - 1 else None

    for piece, (w_in, w_full) in enumerate(weights):
        size = w_in.shape[0]
        for way, to in ((0, up), (1, down)):
            half = half_at(0, way)
            source = w_in if half is None else w_in.at[pl.ds(half * (size // 2), size // 2)]
            send(source, w_full.at[block_of(piece, y, half)], w_send.at[piece], ring_sem.at[way, 0, piece], {"dp": to})
        send(w_in, w_full.at[block_of(piece, y, None)], w_send.at[piece], part_sem.at[piece], {"dp": partner})
        local(w_in, w_full.at[block_of(piece, y, None)], own_sem.at[piece])

    def relay(step, piece):
        w_full = weights[piece][1]
        for way, to in ((0, up), (1, down)):
            number = lax.rem(y + ring - step - 1, ring) if way == 0 else lax.rem(y + step + 1, ring)
            came = w_full.at[block_of(piece, number, half_at(step, way))]
            wait(came, ring_sem.at[way, step, piece])
            if step + 1 < hops:
                onward = w_full.at[block_of(piece, number, half_at(step + 1, way))]
                send(onward, onward, w_send.at[piece], ring_sem.at[way, step + 1, piece], {"dp": to})
            send(came, came, w_send.at[piece], part_sem.at[piece], {"dp": partner})

    pending = [(step, piece) for step in range(hops) for piece in range(3)]

    def pump(count):
        for _ in range(count):
            if pending:
                relay(*pending.pop(0))

    metabuf[GROUP + x] = meta_in[...]
    wait(metabuf.at[pl.ds(0, 2 * GROUP - 1)], meta_sem)
    number = lax.broadcasted_iota(jnp.int32, (experts, rows), 0).astype(F32)
    earlier = (
        lax.broadcasted_iota(jnp.int32, (rows, rows), 0) < lax.broadcasted_iota(jnp.int32, (rows, rows), 1)
    ).astype(BF)
    capacity = cap_in[...]
    first = jnp.where(z > 0, 1.0, 0.0)
    for b in range(GROUP):
        block = metabuf[GROUP + b]
        lanes = pl.ds(b * rows, rows)
        chosen = [(block[k : k + 1, :] == number).astype(F32) for k in range(TOP)]
        before = jnp.dot((chosen[0] + chosen[1]).astype(BF), earlier, preferred_element_type=F32)
        for k in range(TOP):
            rank = jnp.sum(chosen[k] * before, axis=0, keepdims=True)
            limit = jnp.sum(chosen[k] * capacity, axis=0, keepdims=True)
            key = jnp.where(rank < limit, block[k : k + 1, :] * slots + b * MOST + rank, -1.0)
            keyrow[pl.ds(k, 1), lanes] = key
        keyrow[pl.ds(2, 3), lanes] = block[2:5, :]
        docrow[pl.ds(0, 1), pl.ds(span + b * rows, rows)] = block[4:5, :]
        docrow[pl.ds(0, 1), lanes] = (metabuf[b, pl.ds(4, 1), :] + 1.0) * first - 1.0
        keycol[pl.ds(b * rows, rows), :] = jnp.transpose(keyrow[:, lanes])

    batch = min(8, experts)
    part = batch * slots

    def build_pick(g, carry):
        there = at(g * part, part, slots)
        row = (lax.broadcasted_iota(jnp.int32, (part, span), 0) + g * part).astype(F32)
        hit = (row == keyrow[0:1, :]) | (row == keyrow[1:2, :])
        pick[there, :] = hit.astype(F32).astype(BF)
        return carry

    lax.fori_loop(0, experts // batch, build_pick, 0)

    def build_mix(b, carry):
        there = at(b * rows, rows, rows)
        slot = lax.broadcasted_iota(jnp.int32, (rows, experts * slots), 1).astype(F32)
        info = keycol[there, :]
        weight = jnp.where(slot == info[:, 0:1], info[:, 2:3], 0.0) + jnp.where(slot == info[:, 1:2], info[:, 3:4], 0.0)
        mix[there, :] = weight.astype(BF)
        return carry

    lax.fori_loop(0, GROUP, build_mix, 0)

    for c in range(CHUNKS):
        here = pl.ds(c * chunk, chunk)
        wait(kbuf.at[:, here], kv_sem.at[c])
        for buf in (kbuf, vbuf):
            send(
                buf.at[pl.ds(span, span), here],
                buf.at[pl.ds(0, span), here],
                halo_send,
                halo_sem.at[c],
                {"expert": z_next * GROUP + x},
            )
        pump(1)

    near = lax.broadcasted_iota(jnp.int32, (rows, span + rows), 0)
    far = lax.broadcasted_iota(jnp.int32, (rows, span + rows), 1)
    band = (far > near) & (far <= near + span)
    scale = 1.0 / math.sqrt(HEAD_DIM)
    for c in range(CHUNKS):
        here = pl.ds(c * chunk, chunk)
        wait(qbuf.at[:, here], q_sem.at[c])
        wait(kbuf.at[:, here], halo_sem.at[c])

        def attend(b, carry):
            there = at(b * rows, rows, rows)
            reach = at(b * rows, span + rows, rows)
            same = docrow[0:1, reach] == keycol[there, :][:, 4:5]
            bias = jnp.where(band & same, 0.0, -1e30)
            for h in range(heads):
                lanes = pl.ds(c * chunk + h * HEAD_DIM, HEAD_DIM)
                scores = lax.dot_general(
                    qbuf[there, lanes], kbuf[reach, lanes], (((1,), (1,)), ((), ())), preferred_element_type=F32
                )
                scores = scores * scale + bias
                expo = jnp.exp(scores - jnp.max(scores, axis=-1, keepdims=True))
                probs = (expo * (1.0 / jnp.sum(expo, axis=-1, keepdims=True))).astype(BF)
                att[there, lanes] = jnp.dot(probs, vbuf[reach, lanes], preferred_element_type=F32).astype(BF)
            return carry

        lax.fori_loop(0, GROUP, attend, 0)

        def select(g, carry):
            there = at(g * part, part, slots)
            sbuf[there, here] = jnp.dot(pick[there, :], att[:, here], preferred_element_type=F32).astype(BF)
            return carry

        lax.fori_loop(0, experts // batch, select, 0)
        pump(1)
        landing = xbuf.at[at(z * slots, slots, slots), at(x * cols + c * chunk, chunk, HEAD_DIM)]

        def dispatch(i, carry):
            e = lax.rem(me + i, experts)
            send(sbuf.at[at(e * slots, slots, slots), here], landing, disp_send, disp_sem.at[c], {"expert": e})
            return carry

        lax.fori_loop(1, experts, dispatch, 0)
        local(sbuf.at[at(me * slots, slots, slots), here], landing, disp_sem.at[c])

    pump(len(pending))
    for c in range(CHUNKS):
        wait(rbuf.at[:, pl.ds(c * chunk, chunk)], disp_sem.at[c])

    gain = gain_in[...]

    def normalise(g, carry):
        there = at(g * slots, slots, slots)
        row = xbuf[there, :].astype(F32)
        inverse = lax.rsqrt(jnp.sum(row * row, axis=-1, keepdims=True) * (1.0 / width) + 1e-05)
        xbuf[there, :] = (row * inverse * gain).astype(BF)
        return carry

    lax.fori_loop(0, planes, normalise, 0)
    for piece in range(2):
        wait(weights[piece][0], own_sem.at[piece])
        wait(weights[piece][1].at[pl.ds(0, width // 2)], part_sem.at[piece])
    hidden = wgf.shape[1]
    strip = min(256, hidden)

    def inner(n, carry):
        there = at(n * strip, strip, strip)
        gate = jnp.dot(xbuf[...], wgf[:, there], preferred_element_type=F32)
        upward = jnp.dot(xbuf[...], wuf[:, there], preferred_element_type=F32)
        hbuf[:, there] = (gate / (1.0 + jnp.exp(-gate)) * upward).astype(BF)
        return carry

    lax.fori_loop(0, hidden // strip, inner, 0)
    wait(wd_in, own_sem.at[2])
    wait(wdf.at[pl.ds(0, hidden // 2)], part_sem.at[2])

    for c in range(CHUNKS):
        here = pl.ds(c * chunk, chunk)
        landing = rbuf.at[at(me * slots, slots, slots), here]

        def outer(j, carry):
            peer = lax.rem(x + 1 + j, GROUP)
            theirs = at(peer * cols + c * chunk, chunk, HEAD_DIM)
            ybuf[:, theirs] = jnp.dot(hbuf[...], wdf[:, theirs], preferred_element_type=F32).astype(BF)

            def give(i, inner_carry):
                plane = lax.rem(z + i, planes)
                e = plane * GROUP + peer
                source = ybuf.at[at(plane * slots, slots, slots), theirs]

                @pl.when(e != me)
                def _():
                    send(source, landing, ret_send, ret_sem.at[c], {"expert": e})

                @pl.when(e == me)
                def _():
                    local(source, landing, ret_sem.at[c])

                return inner_carry

            lax.fori_loop(0, planes, give, 0)
            return carry

        lax.fori_loop(0, GROUP, outer, 0)

    for c in range(CHUNKS):
        here = pl.ds(c * chunk, chunk)
        wait(rbuf.at[:, here], ret_sem.at[c])

        def combine(b, carry):
            there = at(b * rows, rows, rows)
            total = att[there, here].astype(F32) + jnp.dot(mix[there, :], rbuf[:, here], preferred_element_type=F32)
            fbuf[there, here] = total.astype(BF)
            return carry

        lax.fori_loop(0, GROUP, combine, 0)
        landing = out.at[:, at(x * cols + c * chunk, chunk, HEAD_DIM)]
        for i in range(1, GROUP):
            peer = lax.rem(x + i, GROUP)
            send(
                fbuf.at[at(peer * rows, rows, rows), here], landing, fin_send, fin_sem, {"expert": z * GROUP + peer}
            )
        local(fbuf.at[at(x * rows, rows, rows), here], landing, fin_sem)

    for i in range(3):
        wait(qbuf.at[pl.ds(0, span - rows), :], qkv_send.at[i])
        size = weights[i][0].shape[0]
        wait(weights[i][1].at[pl.ds(0, (dp - 1) * size)], w_send.at[i])
    wait(kbuf, halo_send)
    wait(metabuf.at[pl.ds(0, 2 * GROUP - 1)], meta_send)
    wait(rbuf.at[pl.ds(0, (experts - 1) * slots), :], disp_send)
    wait(rbuf.at[pl.ds(0, (experts - 1) * slots), :], ret_send)
    wait(qbuf.at[pl.ds(0, span - rows), :], fin_send)
    wait(out, fin_sem)


def per_device(
    experts,
    dp,
    queries,
    keys,
    values,
    doc_ids,
    expert_index,
    gates,
    capacity,
    norm_gain,
    gate_weight,
    up_weight,
    down_weight,
):
    rows, width = queries.shape[1:]
    hidden = gate_weight.shape[2]
    cols = width // GROUP
    span = GROUP * rows
    slots = GROUP * MOST
    meta = jnp.concatenate(
        [
            expert_index[0].T.astype(F32),
            gates[0].T,
            doc_ids.astype(F32),
            jnp.zeros((8 - 2 * TOP - 1, rows), F32),
        ],
        axis=0,
    )
    limits = jnp.broadcast_to(capacity.astype(F32)[:, None], (experts, rows))
    hbm = pl.BlockSpec(memory_space=pl.ANY)
    vmem = pl.BlockSpec(memory_space=pltpu.VMEM)
    dma = pltpu.SemaphoreType.DMA
    out = pl.pallas_call(
        functools.partial(layer_kernel, experts, dp),
        out_shape=jax.ShapeDtypeStruct((rows, width), BF),
        in_specs=[hbm, hbm, hbm, vmem, vmem, vmem, hbm, hbm, hbm],
        out_specs=hbm,
        scratch_shapes=[
            pltpu.VMEM((span, cols), BF),
            pltpu.VMEM((2 * span, cols), BF),
            pltpu.VMEM((2 * span, cols), BF),
            pltpu.VMEM((2 * GROUP, 8, rows), F32),
            pltpu.VMEM((8, span), F32),
            pltpu.VMEM((span, 8), F32),
            pltpu.VMEM((8, 2 * span), F32),
            pltpu.VMEM((experts * slots, span), BF),
            pltpu.VMEM((span, experts * slots), BF),
            pltpu.VMEM((span, cols), BF),
            pltpu.VMEM((experts * slots, cols), BF),
            pltpu.VMEM((experts // GROUP * slots, width), BF),
            pltpu.VMEM((experts // GROUP * slots, hidden), BF),
            pltpu.VMEM((experts // GROUP * slots, width), BF),
            pltpu.VMEM((experts * slots, cols), BF),
            pltpu.VMEM((span, cols), BF),
            pltpu.VMEM((width, hidden), BF),
            pltpu.VMEM((width, hidden), BF),
            pltpu.VMEM((hidden, width), BF),
            dma((CHUNKS,)),
            dma((CHUNKS,)),
            dma((CHUNKS,)),
            dma,
            dma((CHUNKS,)),
            dma((CHUNKS,)),
            dma,
            dma((2, dp // 4, 3)),
            dma((3,)),
            dma((3,)),
            dma((3,)),
            dma,
            dma,
            dma,
            dma,
            dma,
            dma((3,)),
        ],
        compiler_params=pltpu.CompilerParams(
            collective_id=0, has_side_effects=True, vmem_limit_bytes=56 * 1024 * 1024
        ),
        name="layer",
    )(
        queries[0],
        keys[0],
        values[0],
        meta,
        limits,
        norm_gain[None, :],
        gate_weight[0],
        up_weight[0],
        down_weight[0],
    )
    return out[None]


def solution(mesh):
    placed = (
        P("dp", "expert", None),
        P("dp", "expert", None),
        P("dp", "expert", None),
        P("dp", "expert"),
        P("dp", "expert", None),
        P("dp", "expert", None),
        P(),
        P(),
        P("expert", "dp", None),
        P("expert", "dp", None),
        P("expert", "dp", None),
    )
    body = functools.partial(per_device, mesh.shape["expert"], mesh.shape["dp"])
    return jax.shard_map(body, mesh=mesh, in_specs=placed, out_specs=P("dp", "expert", None), check_vma=False)
```

```python
import functools
import math

import jax
import jax.numpy as jnp
from jax import lax
from jax.experimental import pallas as pl
from jax.experimental.pallas import tpu as pltpu
from jax.sharding import PartitionSpec as P

HEAD_DIM = 128
TOP = 2
GROUP = 4
MOST = 12
MESH = pl.DeviceIdType.MESH
BF = jnp.bfloat16
F32 = jnp.float32


def layer_kernel(
    experts,
    dp,
    q_in,
    k_in,
    v_in,
    index_in,
    gates_in,
    docs_in,
    cap_in,
    gain_in,
    wg_in,
    wu_in,
    wd_in,
    out,
    indexbuf,
    gatebuf,
    docbuf,
    capbuf,
    gainbuf,
    qbuf,
    kbuf,
    vbuf,
    metabuf,
    keyrow,
    keycol,
    docrow,
    pick,
    mix,
    att,
    sbuf,
    xbuf,
    hbuf,
    ybuf,
    rbuf,
    fbuf,
    wgf,
    wuf,
    wdf,
    small_sem,
    q_sem,
    kv_sem,
    halo_sem,
    meta_sem,
    next_sem,
    disp_sem,
    ret_sem,
    fin_sem,
    ring_sem,
    part_sem,
    own_sem,
    qkv_send,
    halo_send,
    meta_send,
    next_send,
    disp_send,
    ret_send,
    fin_send,
    w_send,
    entered,
):
    rows, width = q_in.shape
    cols = width // GROUP
    heads = cols // HEAD_DIM
    span = GROUP * rows
    slots = GROUP * MOST
    planes = experts // GROUP
    ring = dp // 2
    hops = ring // 2

    me = lax.axis_index("expert")
    z, x = lax.div(me, GROUP), lax.rem(me, GROUP)
    d = lax.axis_index("dp")
    y, core = lax.div(d, 2), lax.rem(d, 2)
    above = {"expert": lax.rem(z + 1, planes) * GROUP + x}
    below = {"expert": lax.rem(z + planes - 1, planes) * GROUP + x}
    up = {"dp": lax.rem(y + 1, ring) * 2 + core}
    down = {"dp": lax.rem(y + ring - 1, ring) * 2 + core}
    partner = {"dp": y * 2 + 1 - core}

    def mate(i):
        return lax.rem(x + i, GROUP)

    def in_group(peer):
        return {"expert": z * GROUP + peer}

    def at(start, size, unit):
        return pl.ds(pl.multiple_of(start, unit), size)

    def send(src, dst, send_sem, recv_sem, where):
        pltpu.make_async_remote_copy(
            src_ref=src, dst_ref=dst, send_sem=send_sem, recv_sem=recv_sem, device_id=where, device_id_type=MESH
        ).start()

    def local(src, dst, sem):
        pltpu.make_async_copy(src, dst, sem).start()

    def wait(ref, sem):
        pltpu.make_async_copy(ref, ref, sem).wait()

    barrier = pltpu.get_barrier_semaphore()
    near = [in_group(mate(i)) for i in range(1, GROUP)] + [above, below, up, down, partner]
    for other in near:
        pl.semaphore_signal(barrier, inc=1, device_id=other, device_id_type=MESH)
    small = ((index_in, indexbuf), (gates_in, gatebuf), (docs_in, docbuf), (cap_in, capbuf), (gain_in, gainbuf))
    for i, (source, buf) in enumerate(small):
        local(source, buf, small_sem.at[i])
    for i, (source, buf) in enumerate(small):
        wait(buf, small_sem.at[i])
    metabuf[GROUP + x, pl.ds(0, TOP), :] = indexbuf[...].astype(F32)
    metabuf[GROUP + x, pl.ds(TOP, TOP), :] = gatebuf[...]
    metabuf[GROUP + x, pl.ds(2 * TOP, 1), :] = docbuf[...].astype(F32)
    metabuf[GROUP + x, pl.ds(2 * TOP + 1, 3), :] = jnp.zeros((3, rows), F32)
    pl.semaphore_wait(barrier, len(near))

    own_rows = at(x * rows, rows, rows)
    own_late = at(span + x * rows, rows, rows)

    def head_at(peer, h):
        return at(peer * cols + h * HEAD_DIM, HEAD_DIM, HEAD_DIM)

    def give_keys(h):
        here = pl.ds(h * HEAD_DIM, HEAD_DIM)
        for i in range(1, GROUP):
            peer = mate(i)
            for n, (source, buf) in enumerate(((k_in, kbuf), (v_in, vbuf))):
                send(source.at[:, head_at(peer, h)], buf.at[own_late, here], qkv_send.at[n], kv_sem.at[h], in_group(peer))

    def give_queries(h):
        here = pl.ds(h * HEAD_DIM, HEAD_DIM)
        for i in range(1, GROUP):
            peer = mate(i)
            send(q_in.at[:, head_at(peer, h)], qbuf.at[own_rows, here], qkv_send.at[2], q_sem.at[h], in_group(peer))

    def give_own(h):
        here = pl.ds(h * HEAD_DIM, HEAD_DIM)
        for source, buf in ((k_in, kbuf), (v_in, vbuf)):
            send(source.at[:, head_at(x, h)], buf.at[own_rows, here], halo_send, halo_sem.at[h], above)

    weights = ((wg_in, wgf), (wu_in, wuf), (wd_in, wdf))

    def block_of(piece, number, half):
        size = weights[piece][0].shape[0]
        base = (number * 2 + core) * size
        if half is None:
            return at(base, size, size)
        return at(base + half * (size // 2), size // 2, size // 2)

    def half_at(step, way):
        return way if step == hops - 1 else None

    def begin(piece):
        w_in, w_full = weights[piece]
        size = w_in.shape[0]
        for way, to in ((0, up), (1, down)):
            half = half_at(0, way)
            source = w_in if half is None else w_in.at[pl.ds(half * (size // 2), size // 2)]
            send(source, w_full.at[block_of(piece, y, half)], w_send.at[piece], ring_sem.at[way, 0, piece], to)
        send(w_in, w_full.at[block_of(piece, y, None)], w_send.at[piece], part_sem.at[piece], partner)
        local(w_in, w_full.at[block_of(piece, y, None)], own_sem.at[piece])

    def relay(step, piece):
        w_full = weights[piece][1]
        for way, to in ((0, up), (1, down)):
            number = lax.rem(y + ring - step - 1, ring) if way == 0 else lax.rem(y + step + 1, ring)
            came = w_full.at[block_of(piece, number, half_at(step, way))]
            wait(came, ring_sem.at[way, step, piece])
            if step + 1 < hops:
                onward = w_full.at[block_of(piece, number, half_at(step + 1, way))]
                send(onward, onward, w_send.at[piece], ring_sem.at[way, step + 1, piece], to)
            send(came, came, w_send.at[piece], part_sem.at[piece], partner)

    pending = []
    for step in range(hops + 1):
        if step < hops:
            pending += [(step, 0), (step, 1)]
        if step == 0:
            pending.append(None)
        else:
            pending.append((step - 1, 2))

    def pump(count):
        for _ in range(count):
            if pending:
                event = pending.pop(0)
                if event is None:
                    begin(2)
                else:
                    relay(*event)

    give_keys(0)
    begin(0)
    give_own(0)
    for i in range(1, GROUP):
        mine = metabuf.at[GROUP + x]
        send(mine, mine, meta_send, meta_sem, in_group(mate(i)))
    begin(1)
    for h in range(1, heads):
        give_own(h)
        give_keys(h)
        give_queries(h - 1)
    give_queries(heads - 1)
    for h in range(heads):
        here = pl.ds(h * HEAD_DIM, HEAD_DIM)
        for source, buf, there, sem in (
            (k_in, kbuf, own_late, kv_sem),
            (v_in, vbuf, own_late, kv_sem),
            (q_in, qbuf, own_rows, q_sem),
        ):
            local(source.at[:, head_at(x, h)], buf.at[there, here], sem.at[h])

    for _ in range(planes // 2):
        pl.semaphore_signal(entered.at[0], inc=1, device_id=above, device_id_type=MESH)
        pl.semaphore_signal(entered.at[1], inc=1, device_id=below, device_id_type=MESH)
        pl.semaphore_wait(entered.at[0], 1)
        pl.semaphore_wait(entered.at[1], 1)

    def forward(h):
        here = pl.ds(h * HEAD_DIM, HEAD_DIM)
        wait(kbuf.at[:, here], kv_sem.at[h])
        for i in range(1, GROUP):
            peer = mate(i)
            for buf in (kbuf, vbuf):
                source = buf.at[at(span + peer * rows, rows, rows), here]
                send(source, buf.at[at(peer * rows, rows, rows), here], halo_send, halo_sem.at[h], above)

    forward(0)

    wait(metabuf.at[pl.ds(0, GROUP - 1)], meta_sem)
    send(metabuf.at[pl.ds(GROUP, GROUP)], metabuf.at[pl.ds(0, GROUP)], next_send, next_sem, above)
    number = lax.broadcasted_iota(jnp.int32, (experts, rows), 0).astype(F32)
    earlier = (
        lax.broadcasted_iota(jnp.int32, (rows, rows), 0) < lax.broadcasted_iota(jnp.int32, (rows, rows), 1)
    ).astype(BF)
    capacity = jnp.broadcast_to(capbuf[...].astype(F32), (8, experts)).astype(BF)
    for b in range(GROUP):
        block = metabuf[GROUP + b]
        lanes = pl.ds(b * rows, rows)
        chosen = [(block[k : k + 1, :] == number).astype(F32) for k in range(TOP)]
        before = jnp.dot((chosen[0] + chosen[1]).astype(BF), earlier, preferred_element_type=F32)
        for k in range(TOP):
            rank = jnp.sum(chosen[k] * before, axis=0, keepdims=True)
            limit = jnp.dot(capacity, chosen[k].astype(BF), preferred_element_type=F32)[0:1, :]
            key = jnp.where(rank < limit, block[k : k + 1, :] * slots + b * MOST + rank, -1.0)
            keyrow[pl.ds(k, 1), lanes] = key
        keyrow[pl.ds(2, 6), lanes] = block[2:8, :]
        docrow[pl.ds(0, 1), pl.ds(span + b * rows, rows)] = block[4:5, :]
        keycol[pl.ds(b * rows, rows), :] = jnp.transpose(keyrow[:, lanes])
    if heads > 1:
        forward(1)

    batch = min(8, experts)
    part = batch * slots

    def build_pick(g, carry):
        there = at(g * part, part, slots)
        row = (lax.broadcasted_iota(jnp.int32, (part, span), 0) + g * part).astype(F32)
        hit = (row == keyrow[0:1, :]) | (row == keyrow[1:2, :])
        pick[there, :] = hit.astype(F32).astype(BF)
        return carry

    lax.fori_loop(0, experts // batch, build_pick, 0)
    pump(1)

    def build_mix(b, carry):
        there = at(b * rows, rows, rows)
        slot = lax.broadcasted_iota(jnp.int32, (rows, experts * slots), 1).astype(F32)
        info = keycol[there, :]
        weight = jnp.where(slot == info[:, 0:1], info[:, 2:3], 0.0) + jnp.where(slot == info[:, 1:2], info[:, 3:4], 0.0)
        mix[there, :] = weight.astype(BF)
        return carry

    lax.fori_loop(0, GROUP, build_mix, 0)
    for h in range(2, heads):
        forward(h)
        pump(1)

    wait(metabuf.at[pl.ds(0, GROUP)], next_sem)
    first = jnp.where(z > 0, 1.0, 0.0)
    for b in range(GROUP):
        docrow[pl.ds(0, 1), pl.ds(b * rows, rows)] = (metabuf[b, pl.ds(4, 1), :] + 1.0) * first - 1.0

    i_row = lax.broadcasted_iota(jnp.int32, (rows, span + rows), 0)
    i_col = lax.broadcasted_iota(jnp.int32, (rows, span + rows), 1)
    band = (i_col > i_row) & (i_col <= i_row + span)
    scale = 1.0 / math.sqrt(HEAD_DIM)
    chunk = max(cols // 2, HEAD_DIM)
    for h in range(heads):
        lanes = pl.ds(h * HEAD_DIM, HEAD_DIM)
        wait(qbuf.at[:, lanes], q_sem.at[h])
        wait(kbuf.at[:, lanes], halo_sem.at[h])

        def attend(b, carry):
            there = at(b * rows, rows, rows)
            reach = at(b * rows, span + rows, rows)
            same = docrow[0:1, reach] == keycol[there, :][:, 4:5]
            bias = jnp.where(band & same, 0.0, -1e30)
            scores = lax.dot_general(
                qbuf[there, lanes], kbuf[reach, lanes], (((1,), (1,)), ((), ())), preferred_element_type=F32
            )
            scores = scores * scale + bias
            expo = jnp.exp(scores - jnp.max(scores, axis=-1, keepdims=True))
            probs = (expo * (1.0 / jnp.sum(expo, axis=-1, keepdims=True))).astype(BF)
            att[there, lanes] = jnp.dot(probs, vbuf[reach, lanes], preferred_element_type=F32).astype(BF)
            return carry

        lax.fori_loop(0, GROUP, attend, 0)
        if (h + 1) * HEAD_DIM % chunk:
            pump(1)
            continue
        c = (h + 1) * HEAD_DIM // chunk - 1
        here = pl.ds(c * chunk, chunk)

        def select(g, carry):
            there = at(g * part, part, slots)
            sbuf[there, here] = jnp.dot(pick[there, :], att[:, here], preferred_element_type=F32).astype(BF)
            return carry

        lax.fori_loop(0, experts // batch, select, 0)
        landing = xbuf.at[at(z * slots, slots, slots), at(x * cols + c * chunk, chunk, HEAD_DIM)]

        def dispatch(i, carry):
            e = lax.rem(me + i, experts)
            send(sbuf.at[at(e * slots, slots, slots), here], landing, disp_send, disp_sem.at[c], {"expert": e})
            return carry

        lax.fori_loop(1, experts, dispatch, 0)
        local(sbuf.at[at(me * slots, slots, slots), here], landing, disp_sem.at[c])
        pump(1)

    pump(len(pending) - 2)
    for c in range(cols // chunk):
        wait(rbuf.at[:, pl.ds(c * chunk, chunk)], disp_sem.at[c])

    gain = gainbuf[...]

    def normalise(g, carry):
        there = at(g * slots, slots, slots)
        row = xbuf[there, :].astype(F32)
        inverse = lax.rsqrt(jnp.sum(row * row, axis=-1, keepdims=True) * (1.0 / width) + 1e-05)
        xbuf[there, :] = (row * inverse * gain).astype(BF)
        return carry

    lax.fori_loop(0, planes, normalise, 0)
    for piece in range(2):
        wait(weights[piece][0], own_sem.at[piece])
        wait(weights[piece][1].at[pl.ds(0, width // 2)], part_sem.at[piece])
    hidden = wgf.shape[1]
    strip = min(256, hidden)

    def inner(n, carry):
        there = at(n * strip, strip, strip)
        gate = jnp.dot(xbuf[...], wgf[:, there], preferred_element_type=F32)
        upward = jnp.dot(xbuf[...], wuf[:, there], preferred_element_type=F32)
        hbuf[:, there] = (gate / (1.0 + jnp.exp(-gate)) * upward).astype(BF)
        return carry

    pump(1)
    strips = hidden // strip
    lax.fori_loop(0, strips - strips // 2, inner, 0)
    pump(len(pending))
    lax.fori_loop(strips - strips // 2, strips, inner, 0)
    wait(wd_in, own_sem.at[2])
    wait(wdf.at[pl.ds(0, hidden // 2)], part_sem.at[2])

    returns, start = [], 0
    while start < cols:
        size = max(HEAD_DIM, (cols // 2 if start == 0 else cols // 4) // HEAD_DIM * HEAD_DIM)
        returns.append((start, size))
        start += size
    for c, (start, size) in enumerate(returns):
        landing = rbuf.at[at(me * slots, slots, slots), pl.ds(start, size)]

        def outer(j, carry):
            peer = mate(1 + j)
            theirs = at(peer * cols + start, size, HEAD_DIM)
            ybuf[:, theirs] = jnp.dot(hbuf[...], wdf[:, theirs], preferred_element_type=F32).astype(BF)

            def give(i, inner_carry):
                plane = lax.rem(z + i, planes)
                e = plane * GROUP + peer
                source = ybuf.at[at(plane * slots, slots, slots), theirs]

                @pl.when(e != me)
                def _():
                    send(source, landing, ret_send, ret_sem.at[c], {"expert": e})

                @pl.when(e == me)
                def _():
                    local(source, landing, ret_sem.at[c])

                return inner_carry

            lax.fori_loop(0, planes, give, 0)
            return carry

        lax.fori_loop(0, GROUP, outer, 0)

    for c, (start, size) in enumerate(returns):
        here = pl.ds(start, size)
        wait(rbuf.at[:, here], ret_sem.at[c])
        landing = out.at[:, at(x * cols + start, size, HEAD_DIM)]

        def combine(j, carry):
            peer = mate(1 + j)
            there = at(peer * rows, rows, rows)
            total = att[there, here].astype(F32) + jnp.dot(mix[there, :], rbuf[:, here], preferred_element_type=F32)
            fbuf[there, here] = total.astype(BF)
            return carry

        lax.fori_loop(0, GROUP, combine, 0)
        for i in range(1, GROUP):
            peer = mate(i)
            send(fbuf.at[at(peer * rows, rows, rows), here], landing, fin_send, fin_sem, in_group(peer))
        local(fbuf.at[own_rows, here], landing, fin_sem)

    for i in range(3):
        wait(qbuf.at[pl.ds(0, span - rows), :], qkv_send.at[i])
        size = weights[i][0].shape[0]
        wait(weights[i][1].at[pl.ds(0, (dp - 1) * size)], w_send.at[i])
    wait(kbuf, halo_send)
    wait(metabuf.at[pl.ds(0, GROUP - 1)], meta_send)
    wait(metabuf.at[pl.ds(0, GROUP)], next_send)
    wait(rbuf.at[pl.ds(0, (experts - 1) * slots), :], disp_send)
    wait(rbuf.at[pl.ds(0, (experts - 1) * slots), :], ret_send)
    wait(qbuf.at[pl.ds(0, span - rows), :], fin_send)
    wait(out, fin_sem)


def per_device(
    experts,
    dp,
    queries,
    keys,
    values,
    doc_ids,
    expert_index,
    gates,
    capacity,
    norm_gain,
    gate_weight,
    up_weight,
    down_weight,
):
    rows, width = queries.shape[1:]
    hidden = gate_weight.shape[2]
    cols = width // GROUP
    span = GROUP * rows
    slots = GROUP * MOST
    heads = cols // HEAD_DIM
    hbm = pl.BlockSpec(memory_space=pl.ANY)
    dma = pltpu.SemaphoreType.DMA
    out = pl.pallas_call(
        functools.partial(layer_kernel, experts, dp),
        out_shape=jax.ShapeDtypeStruct((rows, width), BF),
        in_specs=[hbm] * 11,
        out_specs=hbm,
        scratch_shapes=[
            pltpu.VMEM((TOP, rows), jnp.int32),
            pltpu.VMEM((TOP, rows), F32),
            pltpu.VMEM((1, rows), jnp.int32),
            pltpu.VMEM((1, experts), jnp.int32),
            pltpu.VMEM((1, width), F32),
            pltpu.VMEM((span, cols), BF),
            pltpu.VMEM((2 * span, cols), BF),
            pltpu.VMEM((2 * span, cols), BF),
            pltpu.VMEM((2 * GROUP, 8, rows), F32),
            pltpu.VMEM((8, span), F32),
            pltpu.VMEM((span, 8), F32),
            pltpu.VMEM((8, 2 * span), F32),
            pltpu.VMEM((experts * slots, span), BF),
            pltpu.VMEM((span, experts * slots), BF),
            pltpu.VMEM((span, cols), BF),
            pltpu.VMEM((experts * slots, cols), BF),
            pltpu.VMEM((experts // GROUP * slots, width), BF),
            pltpu.VMEM((experts // GROUP * slots, hidden), BF),
            pltpu.VMEM((experts // GROUP * slots, width), BF),
            pltpu.VMEM((experts * slots, cols), BF),
            pltpu.VMEM((span, cols), BF),
            pltpu.VMEM((width, hidden), BF),
            pltpu.VMEM((width, hidden), BF),
            pltpu.VMEM((hidden, width), BF),
            dma((5,)),
            dma((heads,)),
            dma((heads,)),
            dma((heads,)),
            dma,
            dma,
            dma((2,)),
            dma((4,)),
            dma,
            dma((2, dp // 4, 3)),
            dma((3,)),
            dma((3,)),
            dma((3,)),
            dma,
            dma,
            dma,
            dma,
            dma,
            dma,
            dma((3,)),
            pltpu.SemaphoreType.REGULAR((2,)),
        ],
        compiler_params=pltpu.CompilerParams(
            collective_id=0, has_side_effects=True, vmem_limit_bytes=56 * 1024 * 1024
        ),
        name="layer",
    )(
        queries[0],
        keys[0],
        values[0],
        expert_index[0].T,
        gates[0].T,
        doc_ids,
        capacity[None, :],
        norm_gain[None, :],
        gate_weight[0],
        up_weight[0],
        down_weight[0],
    )
    return out[None]


def solution(mesh):
    placed = (
        P("dp", "expert", None),
        P("dp", "expert", None),
        P("dp", "expert", None),
        P("dp", "expert"),
        P("dp", "expert", None),
        P("dp", "expert", None),
        P(),
        P(),
        P("expert", "dp", None),
        P("expert", "dp", None),
        P("expert", "dp", None),
    )
    body = functools.partial(per_device, mesh.shape["expert"], mesh.shape["dp"])
    return jax.shard_map(body, mesh=mesh, in_specs=placed, out_specs=P("dp", "expert", None), check_vma=False)
```

```python
import functools
import math

import jax
import jax.numpy as jnp
from jax import lax
from jax.experimental import pallas as pl
from jax.experimental.pallas import tpu as pltpu
from jax.sharding import PartitionSpec as P

HEAD_DIM = 128
TOP = 2
GROUP = 4
MOST = 12
MESH = pl.DeviceIdType.MESH
BF = jnp.bfloat16
F32 = jnp.float32


def layer_kernel(
    experts,
    dp,
    q_in,
    k_in,
    v_in,
    index_in,
    gates_in,
    docs_in,
    cap_in,
    gain_in,
    wg_in,
    wu_in,
    wd_in,
    out,
    indexbuf,
    gatebuf,
    docbuf,
    capbuf,
    gainbuf,
    qbuf,
    kbuf,
    vbuf,
    metabuf,
    keyrow,
    keycol,
    docrow,
    pick,
    mix,
    att,
    sbuf,
    xbuf,
    hbuf,
    ybuf,
    rbuf,
    fbuf,
    wgf,
    wuf,
    wdf,
    small_sem,
    q_sem,
    kv_sem,
    halo_sem,
    meta_sem,
    next_sem,
    disp_sem,
    ret_sem,
    fin_sem,
    ring_sem,
    part_sem,
    own_sem,
    qkv_send,
    halo_send,
    meta_send,
    next_send,
    disp_send,
    ret_send,
    fin_send,
    w_send,
    entered,
):
    rows, width = q_in.shape
    cols = width // GROUP
    heads = cols // HEAD_DIM
    span = GROUP * rows
    slots = GROUP * MOST
    planes = experts // GROUP
    ring = dp // 2
    hops = ring // 2

    me = lax.axis_index("expert")
    z, x = lax.div(me, GROUP), lax.rem(me, GROUP)
    d = lax.axis_index("dp")
    y, core = lax.div(d, 2), lax.rem(d, 2)
    above = {"expert": lax.rem(z + 1, planes) * GROUP + x}
    below = {"expert": lax.rem(z + planes - 1, planes) * GROUP + x}
    up = {"dp": lax.rem(y + 1, ring) * 2 + core}
    down = {"dp": lax.rem(y + ring - 1, ring) * 2 + core}
    partner = {"dp": y * 2 + 1 - core}

    def mate(i):
        return lax.rem(x + i, GROUP)

    def in_group(peer):
        return {"expert": z * GROUP + peer}

    def at(start, size, unit):
        return pl.ds(pl.multiple_of(start, unit), size)

    def send(src, dst, send_sem, recv_sem, where):
        pltpu.make_async_remote_copy(
            src_ref=src, dst_ref=dst, send_sem=send_sem, recv_sem=recv_sem, device_id=where, device_id_type=MESH
        ).start()

    def local(src, dst, sem):
        pltpu.make_async_copy(src, dst, sem).start()

    def wait(ref, sem):
        pltpu.make_async_copy(ref, ref, sem).wait()

    barrier = pltpu.get_barrier_semaphore()
    near = [in_group(mate(i)) for i in range(1, GROUP)] + [above, below, up, down, partner]
    for other in near:
        pl.semaphore_signal(barrier, inc=1, device_id=other, device_id_type=MESH)
    small = ((index_in, indexbuf), (gates_in, gatebuf), (docs_in, docbuf), (cap_in, capbuf), (gain_in, gainbuf))
    for i, (source, buf) in enumerate(small):
        local(source, buf, small_sem.at[i])
    for i, (source, buf) in enumerate(small):
        wait(buf, small_sem.at[i])
    metabuf[GROUP + x, pl.ds(0, TOP), :] = indexbuf[...].astype(F32)
    metabuf[GROUP + x, pl.ds(TOP, TOP), :] = gatebuf[...]
    metabuf[GROUP + x, pl.ds(2 * TOP, 1), :] = docbuf[...].astype(F32)
    metabuf[GROUP + x, pl.ds(2 * TOP + 1, 3), :] = jnp.zeros((3, rows), F32)
    pl.semaphore_wait(barrier, len(near))

    own_rows = at(x * rows, rows, rows)
    own_late = at(span + x * rows, rows, rows)

    half_planes = planes // 2

    def offset_of(place):
        turn = planes - 1 - place
        return lax.div(turn + 1, 2) * (2 * lax.rem(turn, 2) - 1)

    def expert_at(i, side):
        place = side * half_planes + lax.rem(i, half_planes)
        plane = lax.rem(z + planes + offset_of(place), planes)
        return place, plane * GROUP + mate(1 + lax.div(i, half_planes))

    def head_at(peer, h):
        return at((h * GROUP + peer) * HEAD_DIM, HEAD_DIM, HEAD_DIM)

    def give_keys(h):
        here = pl.ds(h * HEAD_DIM, HEAD_DIM)
        for i in range(1, GROUP):
            peer = mate(i)
            for n, (source, buf) in enumerate(((k_in, kbuf), (v_in, vbuf))):
                send(source.at[:, head_at(peer, h)], buf.at[own_late, here], qkv_send.at[n], kv_sem.at[h], in_group(peer))

    def give_queries(h):
        here = pl.ds(h * HEAD_DIM, HEAD_DIM)
        for i in range(1, GROUP):
            peer = mate(i)
            send(q_in.at[:, head_at(peer, h)], qbuf.at[own_rows, here], qkv_send.at[2], q_sem.at[h], in_group(peer))

    def give_own(h):
        here = pl.ds(h * HEAD_DIM, HEAD_DIM)
        for source, buf in ((k_in, kbuf), (v_in, vbuf)):
            send(source.at[:, head_at(x, h)], buf.at[own_rows, here], halo_send, halo_sem.at[h], above)

    left, right = pl.ds(0, width // 2), pl.ds(width // 2, width // 2)
    weights = (
        (wg_in, wgf),
        (wu_in, wuf),
        (wd_in.at[:, left], wdf.at[:, left]),
        (wd_in.at[:, right], wdf.at[:, right]),
    )

    def block_of(piece, number, half):
        size = weights[piece][0].shape[0]
        base = (number * 2 + core) * size
        if piece < 2:
            base = (lax.rem(number * 2 + core, GROUP) * heads + lax.div(number * 2 + core, GROUP)) * size
        if half is None:
            return at(base, size, size)
        return at(base + half * (size // 2), size // 2, size // 2)

    def half_at(step, way):
        return way if step == hops - 1 else None

    def begin(piece):
        w_in, w_full = weights[piece]
        size = w_in.shape[0]
        for way, to in ((0, up), (1, down)):
            half = half_at(0, way)
            source = w_in if half is None else w_in.at[pl.ds(half * (size // 2), size // 2)]
            send(source, w_full.at[block_of(piece, y, half)], w_send.at[piece], ring_sem.at[way, 0, piece], to)
        send(w_in, w_full.at[block_of(piece, y, None)], w_send.at[piece], part_sem.at[piece], partner)
        local(w_in, w_full.at[block_of(piece, y, None)], own_sem.at[piece])

    def relay(step, piece):
        w_full = weights[piece][1]
        for way, to in ((0, up), (1, down)):
            number = lax.rem(y + ring - step - 1, ring) if way == 0 else lax.rem(y + step + 1, ring)
            came = w_full.at[block_of(piece, number, half_at(step, way))]
            wait(came, ring_sem.at[way, step, piece])
            if step + 1 < hops:
                onward = w_full.at[block_of(piece, number, half_at(step + 1, way))]
                send(onward, onward, w_send.at[piece], ring_sem.at[way, step + 1, piece], to)
            send(came, came, w_send.at[piece], part_sem.at[piece], partner)

    pending = []
    for step in range(hops):
        pending += [(step, 0), (step, 1)]
        if step == hops - 2:
            pending.append((-1, 3))
        pending.append((step, 2))
        if step == hops - 2:
            pending.append((0, 3))
    pending += [(step, 3) for step in range(1, hops)]

    def pump(count):
        for _ in range(count):
            if pending:
                step, piece = pending.pop(0)
                if step < 0:
                    begin(piece)
                else:
                    relay(step, piece)

    rounds = [planes // 2]

    def announce():
        pl.semaphore_signal(entered.at[0], inc=1, device_id=above, device_id_type=MESH)
        pl.semaphore_signal(entered.at[1], inc=1, device_id=below, device_id_type=MESH)

    def advance():
        if rounds[0] == 0:
            return
        pl.semaphore_wait(entered.at[0], 1)
        pl.semaphore_wait(entered.at[1], 1)
        rounds[0] -= 1
        if rounds[0] > 0:
            announce()

    early = min(2, heads)
    announce()
    give_keys(0)
    begin(0)
    for h in range(heads):
        give_own(h)
    for i in range(1, GROUP):
        mine = metabuf.at[GROUP + x]
        send(mine, mine, meta_send, meta_sem, in_group(mate(i)))
    for h in range(1, early):
        give_keys(h)
    begin(1)
    for h in range(early):
        give_queries(h)
    begin(2)
    for h in range(early, heads):
        give_keys(h)
    for h in range(early, heads):
        give_queries(h)
    for h in range(heads):
        here = pl.ds(h * HEAD_DIM, HEAD_DIM)
        for source, buf, there, sem in (
            (k_in, kbuf, own_late, kv_sem),
            (v_in, vbuf, own_late, kv_sem),
            (q_in, qbuf, own_rows, q_sem),
        ):
            local(source.at[:, head_at(x, h)], buf.at[there, here], sem.at[h])
    advance()

    def forward(h):
        here = pl.ds(h * HEAD_DIM, HEAD_DIM)
        wait(kbuf.at[:, here], kv_sem.at[h])
        for i in range(1, GROUP):
            peer = mate(i)
            for buf in (kbuf, vbuf):
                source = buf.at[at(span + peer * rows, rows, rows), here]
                send(source, buf.at[at(peer * rows, rows, rows), here], halo_send, halo_sem.at[h], above)

    forward(0)
    advance()

    wait(metabuf.at[pl.ds(0, GROUP - 1)], meta_sem)
    send(metabuf.at[pl.ds(GROUP, GROUP)], metabuf.at[pl.ds(0, GROUP)], next_send, next_sem, above)
    number = lax.broadcasted_iota(jnp.int32, (experts, rows), 0).astype(F32)
    earlier = (
        lax.broadcasted_iota(jnp.int32, (rows, rows), 0) < lax.broadcasted_iota(jnp.int32, (rows, rows), 1)
    ).astype(BF)
    capacity = jnp.broadcast_to(capbuf[...].astype(F32), (8, experts)).astype(BF)
    for b in range(GROUP):
        block = metabuf[GROUP + b]
        lanes = pl.ds(b * rows, rows)
        chosen = [(block[k : k + 1, :] == number).astype(F32) for k in range(TOP)]
        before = jnp.dot((chosen[0] + chosen[1]).astype(BF), earlier, preferred_element_type=F32)
        for k in range(TOP):
            rank = jnp.sum(chosen[k] * before, axis=0, keepdims=True)
            limit = jnp.dot(capacity, chosen[k].astype(BF), preferred_element_type=F32)[0:1, :]
            key = jnp.where(rank < limit, block[k : k + 1, :] * slots + b * MOST + rank, -1.0)
            keyrow[pl.ds(k, 1), lanes] = key
        keyrow[pl.ds(2, 6), lanes] = block[2:8, :]
        docrow[pl.ds(0, 1), pl.ds(span + b * rows, rows)] = block[4:5, :]
        keycol[pl.ds(b * rows, rows), :] = jnp.transpose(keyrow[:, lanes])
    for h in range(1, early):
        forward(h)
    pump(1)
    advance()

    batch = min(8, experts)
    part = batch * slots

    def build_pick(g, carry):
        there = at(g * part, part, slots)
        row = (lax.broadcasted_iota(jnp.int32, (part, span), 0) + g * part).astype(F32)
        hit = (row == keyrow[0:1, :]) | (row == keyrow[1:2, :])
        pick[there, :] = hit.astype(F32).astype(BF)
        return carry

    lax.fori_loop(0, experts // batch, build_pick, 0)

    def build_mix(b, carry):
        there = at(b * rows, rows, rows)
        slot = lax.broadcasted_iota(jnp.int32, (rows, experts * slots), 1).astype(F32)
        info = keycol[there, :]
        weight = jnp.where(slot == info[:, 0:1], info[:, 2:3], 0.0) + jnp.where(slot == info[:, 1:2], info[:, 3:4], 0.0)
        mix[there, :] = weight.astype(BF)
        return carry

    lax.fori_loop(0, GROUP, build_mix, 0)
    while rounds[0]:
        advance()

    wait(metabuf.at[pl.ds(0, GROUP)], next_sem)
    first = jnp.where(z > 0, 1.0, 0.0)
    for b in range(GROUP):
        docrow[pl.ds(0, 1), pl.ds(b * rows, rows)] = (metabuf[b, pl.ds(4, 1), :] + 1.0) * first - 1.0

    i_row = lax.broadcasted_iota(jnp.int32, (rows, span + rows), 0)
    i_col = lax.broadcasted_iota(jnp.int32, (rows, span + rows), 1)
    band = (i_col > i_row) & (i_col <= i_row + span)
    scale = 1.0 / math.sqrt(HEAD_DIM)
    chunk = max(cols // 2, HEAD_DIM)
    for h in range(heads):
        lanes = pl.ds(h * HEAD_DIM, HEAD_DIM)
        wait(qbuf.at[:, lanes], q_sem.at[h])
        wait(kbuf.at[:, lanes], halo_sem.at[h])

        def attend(b, carry):
            there = at(b * rows, rows, rows)
            reach = at(b * rows, span + rows, rows)
            same = docrow[0:1, reach] == keycol[there, :][:, 4:5]
            bias = jnp.where(band & same, 0.0, -1e30)
            scores = lax.dot_general(
                qbuf[there, lanes], kbuf[reach, lanes], (((1,), (1,)), ((), ())), preferred_element_type=F32
            )
            scores = scores * scale + bias
            expo = jnp.exp(scores - jnp.max(scores, axis=-1, keepdims=True))
            probs = (expo * (1.0 / jnp.sum(expo, axis=-1, keepdims=True))).astype(BF)
            att[there, lanes] = jnp.dot(probs, vbuf[reach, lanes], preferred_element_type=F32).astype(BF)
            return carry

        lax.fori_loop(0, GROUP, attend, 0)
        if 0 < h < heads - 1:
            pump(2)
        if h + early < heads:
            forward(h + early)
        if (h + 1) * HEAD_DIM % chunk:
            continue
        c = (h + 1) * HEAD_DIM // chunk - 1
        here = pl.ds(c * chunk, chunk)

        def select(g, carry):
            there = at(g * part, part, slots)
            sbuf[there, here] = jnp.dot(pick[there, :], att[:, here], preferred_element_type=F32).astype(BF)
            return carry

        lax.fori_loop(0, experts // batch, select, 0)
        last = h + 1 == heads
        for side in (0, 1) if last else (0,):
            for part_of in (c,) if side == 0 else range(c + 1):
                there = pl.ds(part_of * chunk, chunk)
                theirs = at(x * cols + part_of * chunk, chunk, HEAD_DIM)

                def dispatch(i, carry):
                    place, e = expert_at(i, side)
                    send(
                        sbuf.at[at(e * slots, slots, slots), there],
                        xbuf.at[at(place * slots, slots, slots), theirs],
                        disp_send,
                        disp_sem.at[part_of, side],
                        {"expert": e},
                    )
                    return carry

                lax.fori_loop(0, GROUP * half_planes - side, dispatch, 0)
                if side == 1:
                    local(
                        sbuf.at[at(me * slots, slots, slots), there],
                        xbuf.at[pl.ds((planes - 1) * slots, slots), theirs],
                        disp_sem.at[part_of, side],
                    )
        if not last:
            pump(1)

    pump(len(pending) - (hops - 1))

    gain = jnp.concatenate(
        [
            gainbuf[:, pl.ds((h * GROUP + peer) * HEAD_DIM, HEAD_DIM)]
            for peer in range(GROUP)
            for h in range(heads)
        ],
        axis=1,
    )
    hidden = wgf.shape[1]
    strip = min(256, hidden)
    part_rows = half_planes * slots

    def receive(side):
        for c in range(cols // chunk):
            wait(rbuf.at[pl.ds(0, experts // 2 * slots), pl.ds(c * chunk, chunk)], disp_sem.at[c, side])

        def normalise(g, carry):
            there = at(g * slots, slots, slots)
            row = xbuf[there, :].astype(F32)
            inverse = lax.rsqrt(jnp.sum(row * row, axis=-1, keepdims=True) * (1.0 / width) + 1e-05)
            xbuf[there, :] = (row * inverse * gain).astype(BF)
            return carry

        lax.fori_loop(side * half_planes, (side + 1) * half_planes, normalise, 0)

    def enter(side):
        mine = pl.ds(side * part_rows, part_rows)

        def inner(n, carry):
            there = at(n * strip, strip, strip)
            gate = jnp.dot(xbuf[mine, :], wgf[:, there], preferred_element_type=F32)
            upward = jnp.dot(xbuf[mine, :], wuf[:, there], preferred_element_type=F32)
            hbuf[mine, there] = (gate / (1.0 + jnp.exp(-gate)) * upward).astype(BF)
            return carry

        strips = hidden // strip
        lax.fori_loop(0, strips - strips // 2, inner, 0)
        pump(1)
        lax.fori_loop(strips - strips // 2, strips, inner, 0)

    split = max(heads // 2, 1)
    returns = [(0, split)] + [(h, 1) for h in range(split, heads)]

    def leave(side, c):
        first_head, count = returns[c]
        start, size = first_head * HEAD_DIM, count * HEAD_DIM
        mine = pl.ds(side * part_rows, part_rows)
        landing = rbuf.at[at(me * slots, slots, slots), pl.ds(start, size)]
        for h in range(first_head, first_head + count):
            block = wdf[:, pl.ds(h * GROUP * HEAD_DIM, GROUP * HEAD_DIM)]
            result = jnp.dot(hbuf[mine, :], block, preferred_element_type=F32).astype(BF)
            for peer in range(GROUP):
                ybuf[mine, pl.ds(peer * cols + h * HEAD_DIM, HEAD_DIM)] = result[:, peer * HEAD_DIM : (peer + 1) * HEAD_DIM]

        def outer(j, carry):
            peer = mate(1 + j)
            theirs = at(peer * cols + start, size, HEAD_DIM)

            def give(i, inner_carry):
                place = side * half_planes + i
                plane = lax.rem(z + planes - offset_of(place), planes)
                e = plane * GROUP + peer
                source = ybuf.at[at(place * slots, slots, slots), theirs]

                @pl.when(e != me)
                def _():
                    send(source, landing, ret_send, ret_sem.at[c], {"expert": e})

                @pl.when(e == me)
                def _():
                    local(source, landing, ret_sem.at[c])

                return inner_carry

            lax.fori_loop(0, half_planes, give, 0)
            return carry

        lax.fori_loop(0, GROUP, outer, 0)

    receive(0)
    for piece in range(2):
        wait(weights[piece][0], own_sem.at[piece])
        wait(weights[piece][1].at[pl.ds(0, width // 2)], part_sem.at[piece])
    enter(0)
    for piece in (2, 3):
        wait(weights[piece][0], own_sem.at[piece])
    wait(wdf.at[pl.ds(0, hidden // 2), left], part_sem.at[2])
    leave(0, 0)
    pump(1)
    receive(1)
    enter(1)
    leave(1, 0)
    pump(len(pending))
    wait(wdf.at[pl.ds(0, hidden // 2), right], part_sem.at[3])
    for c in range(1, len(returns)):
        for side in range(2):
            leave(side, c)

    for c, (first_head, count) in enumerate(returns):
        here = pl.ds(first_head * HEAD_DIM, count * HEAD_DIM)
        finished = [(h, pl.ds(h * HEAD_DIM, HEAD_DIM)) for h in range(first_head, first_head + count)]
        wait(rbuf.at[:, here], ret_sem.at[c])

        def hand_over(peer):
            for h, lanes in finished:
                source = fbuf.at[at(peer * rows, rows, rows), lanes]
                send(source, out.at[:, head_at(x, h)], fin_send, fin_sem, in_group(peer))

        ready = None
        for i in (GROUP // 2, *(n for n in range(1, GROUP) if n != GROUP // 2), 0):
            there = at(mate(i) * rows, rows, rows)
            total = att[there, here].astype(F32) + jnp.dot(mix[there, :], rbuf[:, here], preferred_element_type=F32)
            fbuf[there, here] = total.astype(BF)
            if ready is not None:
                hand_over(ready)
            ready = mate(i)
        for h, lanes in finished:
            local(fbuf.at[own_rows, lanes], out.at[:, head_at(x, h)], fin_sem)

    for i in range(3):
        wait(qbuf.at[pl.ds(0, span - rows), :], qkv_send.at[i])
    for i in range(4):
        size = weights[i][0].shape[0]
        wait(weights[i][1].at[pl.ds(0, (dp - 1) * size)], w_send.at[i])
    wait(kbuf, halo_send)
    wait(metabuf.at[pl.ds(0, GROUP - 1)], meta_send)
    wait(metabuf.at[pl.ds(0, GROUP)], next_send)
    wait(rbuf.at[pl.ds(0, (experts - 1) * slots), :], disp_send)
    wait(rbuf.at[pl.ds(0, (experts - 1) * slots), :], ret_send)
    wait(qbuf.at[pl.ds(0, span - rows), :], fin_send)
    wait(out, fin_sem)


def per_device(
    experts,
    dp,
    queries,
    keys,
    values,
    doc_ids,
    expert_index,
    gates,
    capacity,
    norm_gain,
    gate_weight,
    up_weight,
    down_weight,
):
    rows, width = queries.shape[1:]
    hidden = gate_weight.shape[2]
    cols = width // GROUP
    span = GROUP * rows
    slots = GROUP * MOST
    heads = cols // HEAD_DIM
    hbm = pl.BlockSpec(memory_space=pl.ANY)
    dma = pltpu.SemaphoreType.DMA
    out = pl.pallas_call(
        functools.partial(layer_kernel, experts, dp),
        out_shape=jax.ShapeDtypeStruct((rows, width), BF),
        in_specs=[hbm] * 11,
        out_specs=hbm,
        scratch_shapes=[
            pltpu.VMEM((TOP, rows), jnp.int32),
            pltpu.VMEM((TOP, rows), F32),
            pltpu.VMEM((1, rows), jnp.int32),
            pltpu.VMEM((1, experts), jnp.int32),
            pltpu.VMEM((1, width), F32),
            pltpu.VMEM((span, cols), BF),
            pltpu.VMEM((2 * span, cols), BF),
            pltpu.VMEM((2 * span, cols), BF),
            pltpu.VMEM((2 * GROUP, 8, rows), F32),
            pltpu.VMEM((8, span), F32),
            pltpu.VMEM((span, 8), F32),
            pltpu.VMEM((8, 2 * span), F32),
            pltpu.VMEM((experts * slots, span), BF),
            pltpu.VMEM((span, experts * slots), BF),
            pltpu.VMEM((span, cols), BF),
            pltpu.VMEM((experts * slots, cols), BF),
            pltpu.VMEM((experts // GROUP * slots, width), BF),
            pltpu.VMEM((experts // GROUP * slots, hidden), BF),
            pltpu.VMEM((experts // GROUP * slots, width), BF),
            pltpu.VMEM((experts * slots, cols), BF),
            pltpu.VMEM((span, cols), BF),
            pltpu.VMEM((width, hidden), BF),
            pltpu.VMEM((width, hidden), BF),
            pltpu.VMEM((hidden, width), BF),
            dma((5,)),
            dma((heads,)),
            dma((heads,)),
            dma((heads,)),
            dma,
            dma,
            dma((2, 2)),
            dma((4,)),
            dma,
            dma((2, dp // 4, 4)),
            dma((4,)),
            dma((4,)),
            dma((3,)),
            dma,
            dma,
            dma,
            dma,
            dma,
            dma,
            dma((4,)),
            pltpu.SemaphoreType.REGULAR((2,)),
        ],
        compiler_params=pltpu.CompilerParams(
            collective_id=0, has_side_effects=True, vmem_limit_bytes=56 * 1024 * 1024
        ),
        name="layer",
    )(
        queries[0],
        keys[0],
        values[0],
        expert_index[0].T,
        gates[0].T,
        doc_ids,
        capacity[None, :],
        norm_gain[None, :],
        gate_weight[0],
        up_weight[0],
        down_weight[0],
    )
    return out[None]


def solution(mesh):
    placed = (
        P("dp", "expert", None),
        P("dp", "expert", None),
        P("dp", "expert", None),
        P("dp", "expert"),
        P("dp", "expert", None),
        P("dp", "expert", None),
        P(),
        P(),
        P("expert", "dp", None),
        P("expert", "dp", None),
        P("expert", "dp", None),
    )
    body = functools.partial(per_device, mesh.shape["expert"], mesh.shape["dp"])
    return jax.shard_map(body, mesh=mesh, in_specs=placed, out_specs=P("dp", "expert", None), check_vma=False)
```

```python
import functools
import math

import jax
import jax.numpy as jnp
from jax import lax
from jax.experimental import pallas as pl
from jax.experimental.pallas import tpu as pltpu
from jax.sharding import PartitionSpec as P

HEAD_DIM = 128
TOP = 2
GROUP = 4
MOST = 12
MESH = pl.DeviceIdType.MESH
BF = jnp.bfloat16
F32 = jnp.float32


def layer_kernel(
    experts,
    dp,
    q_in,
    k_in,
    v_in,
    index_in,
    gates_in,
    docs_in,
    cap_in,
    gain_in,
    wg_in,
    wu_in,
    wd_in,
    out,
    indexbuf,
    gatebuf,
    docbuf,
    capbuf,
    gainbuf,
    qbuf,
    kbuf,
    vbuf,
    metabuf,
    keyrow,
    keycol,
    docrow,
    pick,
    mix,
    att,
    sbuf,
    xbuf,
    hbuf,
    ybuf,
    rbuf,
    fbuf,
    wgf,
    wuf,
    wdf,
    small_sem,
    q_sem,
    kv_sem,
    halo_sem,
    meta_sem,
    next_sem,
    disp_sem,
    ret_sem,
    fin_sem,
    ring_sem,
    part_sem,
    own_sem,
    qkv_send,
    halo_send,
    meta_send,
    next_send,
    disp_send,
    ret_send,
    fin_send,
    w_send,
    entered,
):
    rows, width = q_in.shape
    cols = width // GROUP
    heads = cols // HEAD_DIM
    span = GROUP * rows
    slots = GROUP * MOST
    planes = experts // GROUP
    ring = dp // 2
    hops = ring // 2

    me = lax.axis_index("expert")
    z, x = lax.div(me, GROUP), lax.rem(me, GROUP)
    d = lax.axis_index("dp")
    y, core = lax.div(d, 2), lax.rem(d, 2)
    above = {"expert": lax.rem(z + 1, planes) * GROUP + x}
    below = {"expert": lax.rem(z + planes - 1, planes) * GROUP + x}
    up = {"dp": lax.rem(y + 1, ring) * 2 + core}
    down = {"dp": lax.rem(y + ring - 1, ring) * 2 + core}
    partner = {"dp": y * 2 + 1 - core}

    def mate(i):
        return lax.rem(x + i, GROUP)

    def in_group(peer):
        return {"expert": z * GROUP + peer}

    def at(start, size, unit):
        return pl.ds(pl.multiple_of(start, unit), size)

    def send(src, dst, send_sem, recv_sem, where):
        pltpu.make_async_remote_copy(
            src_ref=src, dst_ref=dst, send_sem=send_sem, recv_sem=recv_sem, device_id=where, device_id_type=MESH
        ).start()

    def local(src, dst, sem):
        pltpu.make_async_copy(src, dst, sem).start()

    def wait(ref, sem):
        pltpu.make_async_copy(ref, ref, sem).wait()

    barrier = pltpu.get_barrier_semaphore()
    near = [in_group(mate(i)) for i in range(1, GROUP)] + [above, below, up, down, partner]
    for other in near:
        pl.semaphore_signal(barrier, inc=1, device_id=other, device_id_type=MESH)
    small = ((index_in, indexbuf), (gates_in, gatebuf), (docs_in, docbuf), (cap_in, capbuf), (gain_in, gainbuf))
    for i, (source, buf) in enumerate(small):
        local(source, buf, small_sem.at[i])
    for i, (source, buf) in enumerate(small):
        wait(buf, small_sem.at[i])
    metabuf[GROUP + x, pl.ds(0, TOP), :] = indexbuf[...].astype(F32)
    metabuf[GROUP + x, pl.ds(TOP, TOP), :] = gatebuf[...]
    metabuf[GROUP + x, pl.ds(2 * TOP, 1), :] = docbuf[...].astype(F32)
    metabuf[GROUP + x, pl.ds(2 * TOP + 1, 3), :] = jnp.zeros((3, rows), F32)
    pl.semaphore_wait(barrier, len(near))

    own_rows = at(x * rows, rows, rows)
    own_late = at(span + x * rows, rows, rows)

    half_planes = planes // 2

    def offset_of(place):
        turn = planes - 1 - place
        return lax.div(turn + 1, 2) * (2 * lax.rem(turn, 2) - 1)

    def expert_at(i, side):
        place = side * half_planes + lax.rem(i, half_planes)
        plane = lax.rem(z + planes + offset_of(place), planes)
        return place, plane * GROUP + mate(1 + lax.div(i, half_planes))

    def head_at(peer, h):
        return at((h * GROUP + peer) * HEAD_DIM, HEAD_DIM, HEAD_DIM)

    def give_keys(h):
        here = pl.ds(h * HEAD_DIM, HEAD_DIM)
        for i in range(1, GROUP):
            peer = mate(i)
            for n, (source, buf) in enumerate(((k_in, kbuf), (v_in, vbuf))):
                send(source.at[:, head_at(peer, h)], buf.at[own_late, here], qkv_send.at[n], kv_sem.at[h], in_group(peer))

    def give_queries(h):
        here = pl.ds(h * HEAD_DIM, HEAD_DIM)
        for i in range(1, GROUP):
            peer = mate(i)
            send(q_in.at[:, head_at(peer, h)], qbuf.at[own_rows, here], qkv_send.at[2], q_sem.at[h], in_group(peer))

    def give_own(h):
        here = pl.ds(h * HEAD_DIM, HEAD_DIM)
        for source, buf in ((k_in, kbuf), (v_in, vbuf)):
            send(source.at[:, head_at(x, h)], buf.at[own_rows, here], halo_send, halo_sem.at[h], above)

    left, right = pl.ds(0, width // 2), pl.ds(width // 2, width // 2)
    weights = (
        (wg_in, wgf),
        (wu_in, wuf),
        (wd_in.at[:, left], wdf.at[:, left]),
        (wd_in.at[:, right], wdf.at[:, right]),
    )

    def block_of(piece, number, half):
        size = weights[piece][0].shape[0]
        base = (number * 2 + core) * size
        if piece < 2:
            base = (lax.rem(number * 2 + core, GROUP) * heads + lax.div(number * 2 + core, GROUP)) * size
        if half is None:
            return at(base, size, size)
        return at(base + half * (size // 2), size // 2, size // 2)

    def half_at(step, way):
        return way if step == hops - 1 else None

    def begin(piece):
        w_in, w_full = weights[piece]
        size = w_in.shape[0]
        for way, to in ((0, up), (1, down)):
            half = half_at(0, way)
            source = w_in if half is None else w_in.at[pl.ds(half * (size // 2), size // 2)]
            send(source, w_full.at[block_of(piece, y, half)], w_send.at[piece], ring_sem.at[way, 0, piece], to)
        send(w_in, w_full.at[block_of(piece, y, None)], w_send.at[piece], part_sem.at[piece], partner)
        local(w_in, w_full.at[block_of(piece, y, None)], own_sem.at[piece])

    def relay(step, piece):
        w_full = weights[piece][1]
        for way, to in ((0, up), (1, down)):
            number = lax.rem(y + ring - step - 1, ring) if way == 0 else lax.rem(y + step + 1, ring)
            came = w_full.at[block_of(piece, number, half_at(step, way))]
            wait(came, ring_sem.at[way, step, piece])
            if step + 1 < hops:
                onward = w_full.at[block_of(piece, number, half_at(step + 1, way))]
                send(onward, onward, w_send.at[piece], ring_sem.at[way, step + 1, piece], to)
            send(came, came, w_send.at[piece], part_sem.at[piece], partner)

    pending = []
    for step in range(hops):
        pending += [(step, 0), (step, 1), (step, 2)]
        if step == hops - 2:
            pending.append((-1, 3))
    pending += [(step, 3) for step in range(hops)]

    def pump(count):
        for _ in range(count):
            if pending:
                step, piece = pending.pop(0)
                if step < 0:
                    begin(piece)
                else:
                    relay(step, piece)

    rounds = [planes // 2]

    def announce():
        pl.semaphore_signal(entered.at[0], inc=1, device_id=above, device_id_type=MESH)
        pl.semaphore_signal(entered.at[1], inc=1, device_id=below, device_id_type=MESH)

    def advance():
        if rounds[0] == 0:
            return
        pl.semaphore_wait(entered.at[0], 1)
        pl.semaphore_wait(entered.at[1], 1)
        rounds[0] -= 1
        if rounds[0] > 0:
            announce()

    early = min(2, heads)
    announce()
    give_keys(0)
    begin(0)
    for h in range(heads):
        give_own(h)
    for i in range(1, GROUP):
        mine = metabuf.at[GROUP + x]
        send(mine, mine, meta_send, meta_sem, in_group(mate(i)))
    for h in range(1, early):
        give_keys(h)
    begin(1)
    for h in range(early):
        give_queries(h)
    begin(2)
    for h in range(early, heads):
        give_keys(h)
    for h in range(early, heads):
        give_queries(h)
    for h in range(heads):
        here = pl.ds(h * HEAD_DIM, HEAD_DIM)
        for source, buf, there, sem in (
            (k_in, kbuf, own_late, kv_sem),
            (v_in, vbuf, own_late, kv_sem),
            (q_in, qbuf, own_rows, q_sem),
        ):
            local(source.at[:, head_at(x, h)], buf.at[there, here], sem.at[h])
    advance()

    def forward(h):
        here = pl.ds(h * HEAD_DIM, HEAD_DIM)
        wait(kbuf.at[:, here], kv_sem.at[h])
        for i in range(1, GROUP):
            peer = mate(i)
            for buf in (kbuf, vbuf):
                source = buf.at[at(span + peer * rows, rows, rows), here]
                send(source, buf.at[at(peer * rows, rows, rows), here], halo_send, halo_sem.at[h], above)

    forward(0)
    advance()

    wait(metabuf.at[pl.ds(0, GROUP - 1)], meta_sem)
    send(metabuf.at[pl.ds(GROUP, GROUP)], metabuf.at[pl.ds(0, GROUP)], next_send, next_sem, above)
    number = lax.broadcasted_iota(jnp.int32, (experts, rows), 0).astype(F32)
    earlier = (
        lax.broadcasted_iota(jnp.int32, (rows, rows), 0) < lax.broadcasted_iota(jnp.int32, (rows, rows), 1)
    ).astype(BF)
    capacity = jnp.broadcast_to(capbuf[...].astype(F32), (8, experts)).astype(BF)
    for b in range(GROUP):
        block = metabuf[GROUP + b]
        lanes = pl.ds(b * rows, rows)
        chosen = [(block[k : k + 1, :] == number).astype(F32) for k in range(TOP)]
        before = jnp.dot((chosen[0] + chosen[1]).astype(BF), earlier, preferred_element_type=F32)
        for k in range(TOP):
            rank = jnp.sum(chosen[k] * before, axis=0, keepdims=True)
            limit = jnp.dot(capacity, chosen[k].astype(BF), preferred_element_type=F32)[0:1, :]
            key = jnp.where(rank < limit, block[k : k + 1, :] * slots + b * MOST + rank, -1.0)
            keyrow[pl.ds(k, 1), lanes] = key
        keyrow[pl.ds(2, 6), lanes] = block[2:8, :]
        docrow[pl.ds(0, 1), pl.ds(span + b * rows, rows)] = block[4:5, :]
        keycol[pl.ds(b * rows, rows), :] = jnp.transpose(keyrow[:, lanes])
    for h in range(1, early):
        forward(h)
    pump(1)
    advance()

    batch = min(8, experts)
    part = batch * slots

    def build_pick(g, carry):
        there = at(g * part, part, slots)
        row = (lax.broadcasted_iota(jnp.int32, (part, span), 0) + g * part).astype(F32)
        hit = (row == keyrow[0:1, :]) | (row == keyrow[1:2, :])
        pick[there, :] = hit.astype(F32).astype(BF)
        return carry

    lax.fori_loop(0, experts // batch, build_pick, 0)

    def build_mix(b, carry):
        there = at(b * rows, rows, rows)
        slot = lax.broadcasted_iota(jnp.int32, (rows, experts * slots), 1).astype(F32)
        info = keycol[there, :]
        weight = jnp.where(slot == info[:, 0:1], info[:, 2:3], 0.0) + jnp.where(slot == info[:, 1:2], info[:, 3:4], 0.0)
        mix[there, :] = weight.astype(BF)
        return carry

    lax.fori_loop(0, GROUP, build_mix, 0)
    while rounds[0]:
        advance()

    wait(metabuf.at[pl.ds(0, GROUP)], next_sem)
    first = jnp.where(z > 0, 1.0, 0.0)
    for b in range(GROUP):
        docrow[pl.ds(0, 1), pl.ds(b * rows, rows)] = (metabuf[b, pl.ds(4, 1), :] + 1.0) * first - 1.0

    i_row = lax.broadcasted_iota(jnp.int32, (rows, span + rows), 0)
    i_col = lax.broadcasted_iota(jnp.int32, (rows, span + rows), 1)
    band = (i_col > i_row) & (i_col <= i_row + span)
    scale = 1.0 / math.sqrt(HEAD_DIM)
    chunk = max(cols // 2, HEAD_DIM)
    for h in range(heads):
        lanes = pl.ds(h * HEAD_DIM, HEAD_DIM)
        wait(qbuf.at[:, lanes], q_sem.at[h])
        wait(kbuf.at[:, lanes], halo_sem.at[h])

        def attend(b, carry):
            there = at(b * rows, rows, rows)
            reach = at(b * rows, span + rows, rows)
            same = docrow[0:1, reach] == keycol[there, :][:, 4:5]
            bias = jnp.where(band & same, 0.0, -1e30)
            scores = lax.dot_general(
                qbuf[there, lanes], kbuf[reach, lanes], (((1,), (1,)), ((), ())), preferred_element_type=F32
            )
            scores = scores * scale + bias
            expo = jnp.exp(scores - jnp.max(scores, axis=-1, keepdims=True))
            probs = (expo * (1.0 / jnp.sum(expo, axis=-1, keepdims=True))).astype(BF)
            att[there, lanes] = jnp.dot(probs, vbuf[reach, lanes], preferred_element_type=F32).astype(BF)
            return carry

        lax.fori_loop(0, GROUP, attend, 0)
        if 0 < h < heads - 1:
            pump(2)
        if h + early < heads:
            forward(h + early)
        if (h + 1) * HEAD_DIM % chunk:
            continue
        c = (h + 1) * HEAD_DIM // chunk - 1
        here = pl.ds(c * chunk, chunk)

        def select(g, carry):
            there = at(g * part, part, slots)
            sbuf[there, here] = jnp.dot(pick[there, :], att[:, here], preferred_element_type=F32).astype(BF)
            return carry

        lax.fori_loop(0, experts // batch, select, 0)
        last = h + 1 == heads
        for side in (0, 1) if last else (0,):
            for part_of in (c,) if side == 0 else range(c + 1):
                there = pl.ds(part_of * chunk, chunk)
                theirs = at(x * cols + part_of * chunk, chunk, HEAD_DIM)

                def dispatch(i, carry):
                    place, e = expert_at(i, side)
                    send(
                        sbuf.at[at(e * slots, slots, slots), there],
                        xbuf.at[at(place * slots, slots, slots), theirs],
                        disp_send,
                        disp_sem.at[part_of, side],
                        {"expert": e},
                    )
                    return carry

                lax.fori_loop(0, GROUP * half_planes - side, dispatch, 0)
                if side == 1:
                    local(
                        sbuf.at[at(me * slots, slots, slots), there],
                        xbuf.at[pl.ds((planes - 1) * slots, slots), theirs],
                        disp_sem.at[part_of, side],
                    )
        if not last:
            pump(1)

    pump(len(pending) - hops)

    gain = jnp.concatenate(
        [
            gainbuf[:, pl.ds((h * GROUP + peer) * HEAD_DIM, HEAD_DIM)]
            for peer in range(GROUP)
            for h in range(heads)
        ],
        axis=1,
    )
    hidden = wgf.shape[1]
    strip = min(256, hidden)
    part_rows = half_planes * slots

    def receive(side):
        for c in range(cols // chunk):
            wait(rbuf.at[pl.ds(0, experts // 2 * slots), pl.ds(c * chunk, chunk)], disp_sem.at[c, side])

        def normalise(g, carry):
            there = at(g * slots, slots, slots)
            row = xbuf[there, :].astype(F32)
            inverse = lax.rsqrt(jnp.sum(row * row, axis=-1, keepdims=True) * (1.0 / width) + 1e-05)
            xbuf[there, :] = (row * inverse * gain).astype(BF)
            return carry

        lax.fori_loop(side * half_planes, (side + 1) * half_planes, normalise, 0)

    def enter(side):
        mine = pl.ds(side * part_rows, part_rows)

        def inner(n, carry):
            there = at(n * strip, strip, strip)
            gate = jnp.dot(xbuf[mine, :], wgf[:, there], preferred_element_type=F32)
            upward = jnp.dot(xbuf[mine, :], wuf[:, there], preferred_element_type=F32)
            hbuf[mine, there] = (gate / (1.0 + jnp.exp(-gate)) * upward).astype(BF)
            return carry

        strips = hidden // strip
        lax.fori_loop(0, strips - strips // 2, inner, 0)
        pump(1)
        lax.fori_loop(strips - strips // 2, strips, inner, 0)

    split = max(heads // 2, 1)
    returns = [(0, split)] + [(h, 1) for h in range(split, heads)]

    def leave(side, c):
        first_head, count = returns[c]
        start, size = first_head * HEAD_DIM, count * HEAD_DIM
        mine = pl.ds(side * part_rows, part_rows)
        landing = rbuf.at[at(me * slots, slots, slots), pl.ds(start, size)]
        for h in range(first_head, first_head + count):
            block = wdf[:, pl.ds(h * GROUP * HEAD_DIM, GROUP * HEAD_DIM)]
            result = jnp.dot(hbuf[mine, :], block, preferred_element_type=F32).astype(BF)
            for peer in range(GROUP):
                ybuf[mine, pl.ds(peer * cols + h * HEAD_DIM, HEAD_DIM)] = result[:, peer * HEAD_DIM : (peer + 1) * HEAD_DIM]

        def outer(j, carry):
            peer = mate(1 + j)
            theirs = at(peer * cols + start, size, HEAD_DIM)

            def give(i, inner_carry):
                place = side * half_planes + i
                plane = lax.rem(z + planes - offset_of(place), planes)
                e = plane * GROUP + peer
                source = ybuf.at[at(place * slots, slots, slots), theirs]

                @pl.when(e != me)
                def _():
                    send(source, landing, ret_send, ret_sem.at[c], {"expert": e})

                @pl.when(e == me)
                def _():
                    local(source, landing, ret_sem.at[c])

                return inner_carry

            lax.fori_loop(0, half_planes, give, 0)
            return carry

        lax.fori_loop(0, GROUP, outer, 0)

    receive(0)
    for piece in range(2):
        wait(weights[piece][0], own_sem.at[piece])
        wait(weights[piece][1].at[pl.ds(0, width // 2)], part_sem.at[piece])
    enter(0)
    for piece in (2, 3):
        wait(weights[piece][0], own_sem.at[piece])
    wait(wdf.at[pl.ds(0, hidden // 2), left], part_sem.at[2])
    leave(0, 0)
    pump(1)
    receive(1)
    enter(1)
    leave(1, 0)
    pump(len(pending))
    wait(wdf.at[pl.ds(0, hidden // 2), right], part_sem.at[3])
    for c in range(1, len(returns)):
        for side in range(2):
            leave(side, c)

    for c, (first_head, count) in enumerate(returns):
        here = pl.ds(first_head * HEAD_DIM, count * HEAD_DIM)
        finished = [(h, pl.ds(h * HEAD_DIM, HEAD_DIM)) for h in range(first_head, first_head + count)]
        wait(rbuf.at[:, here], ret_sem.at[c])

        def hand_over(peer):
            for h, lanes in finished:
                source = fbuf.at[at(peer * rows, rows, rows), lanes]
                send(source, out.at[:, head_at(x, h)], fin_send, fin_sem, in_group(peer))

        ready = None
        for i in (GROUP // 2, *(n for n in range(1, GROUP) if n != GROUP // 2), 0):
            there = at(mate(i) * rows, rows, rows)
            total = att[there, here].astype(F32) + jnp.dot(mix[there, :], rbuf[:, here], preferred_element_type=F32)
            fbuf[there, here] = total.astype(BF)
            if ready is not None:
                hand_over(ready)
            ready = mate(i)
        for h, lanes in finished:
            local(fbuf.at[own_rows, lanes], out.at[:, head_at(x, h)], fin_sem)

    for i in range(3):
        wait(qbuf.at[pl.ds(0, span - rows), :], qkv_send.at[i])
    for i in range(4):
        size = weights[i][0].shape[0]
        wait(weights[i][1].at[pl.ds(0, (dp - 1) * size)], w_send.at[i])
    wait(kbuf, halo_send)
    wait(metabuf.at[pl.ds(0, GROUP - 1)], meta_send)
    wait(metabuf.at[pl.ds(0, GROUP)], next_send)
    wait(rbuf.at[pl.ds(0, (experts - 1) * slots), :], disp_send)
    wait(rbuf.at[pl.ds(0, (experts - 1) * slots), :], ret_send)
    wait(qbuf.at[pl.ds(0, span - rows), :], fin_send)
    wait(out, fin_sem)


def per_device(
    experts,
    dp,
    queries,
    keys,
    values,
    doc_ids,
    expert_index,
    gates,
    capacity,
    norm_gain,
    gate_weight,
    up_weight,
    down_weight,
):
    rows, width = queries.shape[1:]
    hidden = gate_weight.shape[2]
    cols = width // GROUP
    span = GROUP * rows
    slots = GROUP * MOST
    heads = cols // HEAD_DIM
    hbm = pl.BlockSpec(memory_space=pl.ANY)
    dma = pltpu.SemaphoreType.DMA
    out = pl.pallas_call(
        functools.partial(layer_kernel, experts, dp),
        out_shape=pltpu.VMEM((rows, width), BF),
        in_specs=[hbm] * 11,
        out_specs=pl.BlockSpec(memory_space=pltpu.VMEM),
        scratch_shapes=[
            pltpu.VMEM((TOP, rows), jnp.int32),
            pltpu.VMEM((TOP, rows), F32),
            pltpu.VMEM((1, rows), jnp.int32),
            pltpu.VMEM((1, experts), jnp.int32),
            pltpu.VMEM((1, width), F32),
            pltpu.VMEM((span, cols), BF),
            pltpu.VMEM((2 * span, cols), BF),
            pltpu.VMEM((2 * span, cols), BF),
            pltpu.VMEM((2 * GROUP, 8, rows), F32),
            pltpu.VMEM((8, span), F32),
            pltpu.VMEM((span, 8), F32),
            pltpu.VMEM((8, 2 * span), F32),
            pltpu.VMEM((experts * slots, span), BF),
            pltpu.VMEM((span, experts * slots), BF),
            pltpu.VMEM((span, cols), BF),
            pltpu.VMEM((experts * slots, cols), BF),
            pltpu.VMEM((experts // GROUP * slots, width), BF),
            pltpu.VMEM((experts // GROUP * slots, hidden), BF),
            pltpu.VMEM((experts // GROUP * slots, width), BF),
            pltpu.VMEM((experts * slots, cols), BF),
            pltpu.VMEM((span, cols), BF),
            pltpu.VMEM((width, hidden), BF),
            pltpu.VMEM((width, hidden), BF),
            pltpu.VMEM((hidden, width), BF),
            dma((5,)),
            dma((heads,)),
            dma((heads,)),
            dma((heads,)),
            dma,
            dma,
            dma((2, 2)),
            dma((4,)),
            dma,
            dma((2, dp // 4, 4)),
            dma((4,)),
            dma((4,)),
            dma((3,)),
            dma,
            dma,
            dma,
            dma,
            dma,
            dma,
            dma((4,)),
            pltpu.SemaphoreType.REGULAR((2,)),
        ],
        compiler_params=pltpu.CompilerParams(
            collective_id=0, has_side_effects=True, vmem_limit_bytes=56 * 1024 * 1024
        ),
        name="layer",
    )(
        queries[0],
        keys[0],
        values[0],
        expert_index[0].T,
        gates[0].T,
        doc_ids,
        capacity[None, :],
        norm_gain[None, :],
        gate_weight[0],
        up_weight[0],
        down_weight[0],
    )
    return out[None]


def solution(mesh):
    placed = (
        P("dp", "expert", None),
        P("dp", "expert", None),
        P("dp", "expert", None),
        P("dp", "expert"),
        P("dp", "expert", None),
        P("dp", "expert", None),
        P(),
        P(),
        P("expert", "dp", None),
        P("expert", "dp", None),
        P("expert", "dp", None),
    )
    body = functools.partial(per_device, mesh.shape["expert"], mesh.shape["dp"])
    return jax.shard_map(body, mesh=mesh, in_specs=placed, out_specs=P("dp", "expert", None), check_vma=False)
```

```python
import functools
import math

import jax
import jax.numpy as jnp
from jax import lax
from jax.experimental import pallas as pl
from jax.experimental.pallas import tpu as pltpu
from jax.sharding import PartitionSpec as P

HEAD_DIM = 128
TOP = 2
GROUP = 4
MOST = 12
MESH = pl.DeviceIdType.MESH
BF = jnp.bfloat16
F32 = jnp.float32


def layer_kernel(
    experts,
    dp,
    q_in,
    k_in,
    v_in,
    index_in,
    gates_in,
    docs_in,
    cap_in,
    gain_in,
    wg_in,
    wu_in,
    wd_in,
    out,
    indexbuf,
    gatebuf,
    docbuf,
    capbuf,
    gainbuf,
    qbuf,
    kbuf,
    vbuf,
    metabuf,
    keyrow,
    keycol,
    docrow,
    pick,
    mix,
    att,
    sbuf,
    xbuf,
    hbuf,
    ybuf,
    rbuf,
    fbuf,
    wgf,
    wuf,
    wdf,
    small_sem,
    q_sem,
    kv_sem,
    halo_sem,
    meta_sem,
    next_sem,
    disp_sem,
    ret_sem,
    fin_sem,
    ring_sem,
    part_sem,
    own_sem,
    qkv_send,
    halo_send,
    meta_send,
    next_send,
    disp_send,
    ret_send,
    fin_send,
    w_send,
    entered,
):
    rows, width = q_in.shape
    cols = width // GROUP
    heads = cols // HEAD_DIM
    span = GROUP * rows
    slots = GROUP * MOST
    planes = experts // GROUP
    ring = dp // 2
    hops = ring // 2

    me = lax.axis_index("expert")
    z, x = lax.div(me, GROUP), lax.rem(me, GROUP)
    d = lax.axis_index("dp")
    y, core = lax.div(d, 2), lax.rem(d, 2)
    above = {"expert": lax.rem(z + 1, planes) * GROUP + x}
    below = {"expert": lax.rem(z + planes - 1, planes) * GROUP + x}
    up = {"dp": lax.rem(y + 1, ring) * 2 + core}
    down = {"dp": lax.rem(y + ring - 1, ring) * 2 + core}
    partner = {"dp": y * 2 + 1 - core}

    def mate(i):
        return lax.rem(x + i, GROUP)

    def in_group(peer):
        return {"expert": z * GROUP + peer}

    def at(start, size, unit):
        return pl.ds(pl.multiple_of(start, unit), size)

    def send(src, dst, send_sem, recv_sem, where):
        pltpu.make_async_remote_copy(
            src_ref=src, dst_ref=dst, send_sem=send_sem, recv_sem=recv_sem, device_id=where, device_id_type=MESH
        ).start()

    def local(src, dst, sem):
        pltpu.make_async_copy(src, dst, sem).start()

    def wait(ref, sem):
        pltpu.make_async_copy(ref, ref, sem).wait()

    barrier = pltpu.get_barrier_semaphore()
    near = [in_group(mate(i)) for i in range(1, GROUP)] + [above, below, up, down, partner]
    for other in near:
        pl.semaphore_signal(barrier, inc=1, device_id=other, device_id_type=MESH)
    small = ((index_in, indexbuf), (gates_in, gatebuf), (docs_in, docbuf), (cap_in, capbuf), (gain_in, gainbuf))
    for i, (source, buf) in enumerate(small):
        local(source, buf, small_sem.at[i])
    pl.semaphore_wait(barrier, len(near))

    own_rows = at(x * rows, rows, rows)
    own_late = at(span + x * rows, rows, rows)

    half_planes = planes // 2

    def offset_of(place):
        turn = planes - 1 - place
        return lax.div(turn + 1, 2) * (2 * lax.rem(turn, 2) - 1)

    def expert_at(i, side):
        place = side * half_planes + lax.rem(i, half_planes)
        plane = lax.rem(z + planes + offset_of(place), planes)
        return place, plane * GROUP + mate(1 + lax.div(i, half_planes))

    def head_at(peer, h):
        return at((h * GROUP + peer) * HEAD_DIM, HEAD_DIM, HEAD_DIM)

    def give_keys(h):
        here = pl.ds(h * HEAD_DIM, HEAD_DIM)
        for i in range(1, GROUP):
            peer = mate(i)
            for n, (source, buf) in enumerate(((k_in, kbuf), (v_in, vbuf))):
                send(source.at[:, head_at(peer, h)], buf.at[own_late, here], qkv_send.at[n], kv_sem.at[h], in_group(peer))

    def give_queries(h):
        here = pl.ds(h * HEAD_DIM, HEAD_DIM)
        for i in range(1, GROUP):
            peer = mate(i)
            send(q_in.at[:, head_at(peer, h)], qbuf.at[own_rows, here], qkv_send.at[2], q_sem.at[h], in_group(peer))

    def give_own(h):
        here = pl.ds(h * HEAD_DIM, HEAD_DIM)
        for source, buf in ((k_in, kbuf), (v_in, vbuf)):
            send(source.at[:, head_at(x, h)], buf.at[own_rows, here], halo_send, halo_sem.at[h], above)

    left, right = pl.ds(0, width // 2), pl.ds(width // 2, width // 2)
    weights = (
        (wg_in, wgf),
        (wu_in, wuf),
        (wd_in.at[:, left], wdf.at[:, left]),
        (wd_in.at[:, right], wdf.at[:, right]),
    )

    def block_of(piece, number, half):
        size = weights[piece][0].shape[0]
        base = (number * 2 + core) * size
        if piece < 2:
            base = (lax.rem(number * 2 + core, GROUP) * heads + lax.div(number * 2 + core, GROUP)) * size
        if half is None:
            return at(base, size, size)
        return at(base + half * (size // 2), size // 2, size // 2)

    def half_at(step, way):
        return way if step == hops - 1 else None

    def begin(piece):
        w_in, w_full = weights[piece]
        size = w_in.shape[0]
        for way, to in ((0, up), (1, down)):
            half = half_at(0, way)
            source = w_in if half is None else w_in.at[pl.ds(half * (size // 2), size // 2)]
            send(source, w_full.at[block_of(piece, y, half)], w_send.at[piece], ring_sem.at[way, 0, piece], to)
        send(w_in, w_full.at[block_of(piece, y, None)], w_send.at[piece], part_sem.at[piece], partner)
        local(w_in, w_full.at[block_of(piece, y, None)], own_sem.at[piece])

    def relay(step, piece):
        w_full = weights[piece][1]
        for way, to in ((0, up), (1, down)):
            number = lax.rem(y + ring - step - 1, ring) if way == 0 else lax.rem(y + step + 1, ring)
            came = w_full.at[block_of(piece, number, half_at(step, way))]
            wait(came, ring_sem.at[way, step, piece])
            if step + 1 < hops:
                onward = w_full.at[block_of(piece, number, half_at(step + 1, way))]
                send(onward, onward, w_send.at[piece], ring_sem.at[way, step + 1, piece], to)
            send(came, came, w_send.at[piece], part_sem.at[piece], partner)

    pending = []
    for step in range(hops):
        pending += [(step, 0), (step, 1), (step, 2)]
        if step == hops - 2:
            pending.append((-1, 3))
    pending += [(step, 3) for step in range(hops)]

    def pump(count):
        for _ in range(count):
            if pending:
                step, piece = pending.pop(0)
                if step < 0:
                    begin(piece)
                else:
                    relay(step, piece)

    rounds = [planes // 2]

    def announce():
        pl.semaphore_signal(entered.at[0], inc=1, device_id=above, device_id_type=MESH)
        pl.semaphore_signal(entered.at[1], inc=1, device_id=below, device_id_type=MESH)

    def advance():
        if rounds[0] == 0:
            return
        pl.semaphore_wait(entered.at[0], 1)
        pl.semaphore_wait(entered.at[1], 1)
        rounds[0] -= 1
        if rounds[0] > 0:
            announce()

    early = min(2, heads)
    announce()
    begin(0)
    give_keys(0)
    for h in range(heads):
        give_own(h)
    for i, (source, buf) in enumerate(small):
        wait(buf, small_sem.at[i])
    metabuf[GROUP + x, pl.ds(0, TOP), :] = indexbuf[...].astype(F32)
    metabuf[GROUP + x, pl.ds(TOP, TOP), :] = gatebuf[...]
    metabuf[GROUP + x, pl.ds(2 * TOP, 1), :] = docbuf[...].astype(F32)
    metabuf[GROUP + x, pl.ds(2 * TOP + 1, 3), :] = jnp.zeros((3, rows), F32)
    for h in range(1, early):
        give_keys(h)
    begin(1)
    for h in range(early):
        give_queries(h)
    begin(2)
    for h in range(early, heads):
        give_keys(h)
    for h in range(early, heads):
        give_queries(h)
    for i in range(1, GROUP):
        mine = metabuf.at[GROUP + x]
        send(mine, mine, meta_send, meta_sem, in_group(mate(i)))
    for h in range(heads):
        here = pl.ds(h * HEAD_DIM, HEAD_DIM)
        for source, buf, there, sem in (
            (k_in, kbuf, own_late, kv_sem),
            (v_in, vbuf, own_late, kv_sem),
            (q_in, qbuf, own_rows, q_sem),
        ):
            local(source.at[:, head_at(x, h)], buf.at[there, here], sem.at[h])
    advance()

    def forward(h):
        here = pl.ds(h * HEAD_DIM, HEAD_DIM)
        wait(kbuf.at[:, here], kv_sem.at[h])
        for i in range(1, GROUP):
            peer = mate(i)
            for buf in (kbuf, vbuf):
                source = buf.at[at(span + peer * rows, rows, rows), here]
                send(source, buf.at[at(peer * rows, rows, rows), here], halo_send, halo_sem.at[h], above)

    forward(0)
    advance()

    wait(metabuf.at[pl.ds(0, GROUP - 1)], meta_sem)
    send(metabuf.at[pl.ds(GROUP, GROUP)], metabuf.at[pl.ds(0, GROUP)], next_send, next_sem, above)
    number = lax.broadcasted_iota(jnp.int32, (experts, rows), 0).astype(F32)
    earlier = (
        lax.broadcasted_iota(jnp.int32, (rows, rows), 0) < lax.broadcasted_iota(jnp.int32, (rows, rows), 1)
    ).astype(BF)
    capacity = jnp.broadcast_to(capbuf[...].astype(F32), (8, experts)).astype(BF)
    for b in range(GROUP):
        block = metabuf[GROUP + b]
        lanes = pl.ds(b * rows, rows)
        chosen = [(block[k : k + 1, :] == number).astype(F32) for k in range(TOP)]
        before = jnp.dot((chosen[0] + chosen[1]).astype(BF), earlier, preferred_element_type=F32)
        for k in range(TOP):
            rank = jnp.sum(chosen[k] * before, axis=0, keepdims=True)
            limit = jnp.dot(capacity, chosen[k].astype(BF), preferred_element_type=F32)[0:1, :]
            key = jnp.where(rank < limit, block[k : k + 1, :] * slots + b * MOST + rank, -1.0)
            keyrow[pl.ds(k, 1), lanes] = key
        keyrow[pl.ds(2, 6), lanes] = block[2:8, :]
        docrow[pl.ds(0, 1), pl.ds(span + b * rows, rows)] = block[4:5, :]
        keycol[pl.ds(b * rows, rows), :] = jnp.transpose(keyrow[:, lanes])
    for h in range(1, early):
        forward(h)
    pump(1)
    advance()

    batch = min(8, experts)
    part = batch * slots

    def build_pick(g, carry):
        there = at(g * part, part, slots)
        row = (lax.broadcasted_iota(jnp.int32, (part, span), 0) + g * part).astype(F32)
        hit = (row == keyrow[0:1, :]) | (row == keyrow[1:2, :])
        pick[there, :] = hit.astype(F32).astype(BF)
        return carry

    lax.fori_loop(0, experts // batch, build_pick, 0)

    def build_mix(b, carry):
        there = at(b * rows, rows, rows)
        slot = lax.broadcasted_iota(jnp.int32, (rows, experts * slots), 1).astype(F32)
        info = keycol[there, :]
        weight = jnp.where(slot == info[:, 0:1], info[:, 2:3], 0.0) + jnp.where(slot == info[:, 1:2], info[:, 3:4], 0.0)
        mix[there, :] = weight.astype(BF)
        return carry

    lax.fori_loop(0, GROUP, build_mix, 0)
    while rounds[0]:
        advance()

    wait(metabuf.at[pl.ds(0, GROUP)], next_sem)
    first = jnp.where(z > 0, 1.0, 0.0)
    for b in range(GROUP):
        docrow[pl.ds(0, 1), pl.ds(b * rows, rows)] = (metabuf[b, pl.ds(4, 1), :] + 1.0) * first - 1.0

    i_row = lax.broadcasted_iota(jnp.int32, (rows, span + rows), 0)
    i_col = lax.broadcasted_iota(jnp.int32, (rows, span + rows), 1)
    band = (i_col > i_row) & (i_col <= i_row + span)
    scale = 1.0 / math.sqrt(HEAD_DIM)
    chunk = max(cols // 2, HEAD_DIM)
    for h in range(heads):
        lanes = pl.ds(h * HEAD_DIM, HEAD_DIM)
        wait(qbuf.at[:, lanes], q_sem.at[h])
        wait(kbuf.at[:, lanes], halo_sem.at[h])

        def attend(b, carry):
            there = at(b * rows, rows, rows)
            reach = at(b * rows, span + rows, rows)
            same = docrow[0:1, reach] == keycol[there, :][:, 4:5]
            bias = jnp.where(band & same, 0.0, -1e30)
            scores = lax.dot_general(
                qbuf[there, lanes], kbuf[reach, lanes], (((1,), (1,)), ((), ())), preferred_element_type=F32
            )
            scores = scores * scale + bias
            expo = jnp.exp(scores - jnp.max(scores, axis=-1, keepdims=True))
            probs = (expo * (1.0 / jnp.sum(expo, axis=-1, keepdims=True))).astype(BF)
            att[there, lanes] = jnp.dot(probs, vbuf[reach, lanes], preferred_element_type=F32).astype(BF)
            return carry

        lax.fori_loop(0, GROUP, attend, 0)
        if 0 < h < heads - 1:
            pump(2)
        if h + early < heads:
            forward(h + early)
        if (h + 1) * HEAD_DIM % chunk:
            continue
        c = (h + 1) * HEAD_DIM // chunk - 1
        here = pl.ds(c * chunk, chunk)

        def select(g, carry):
            there = at(g * part, part, slots)
            sbuf[there, here] = jnp.dot(pick[there, :], att[:, here], preferred_element_type=F32).astype(BF)
            return carry

        lax.fori_loop(0, experts // batch, select, 0)
        last = h + 1 == heads
        for side in (0, 1) if last else (0,):
            for part_of in (c,) if side == 0 else range(c + 1):
                there = pl.ds(part_of * chunk, chunk)
                theirs = at(x * cols + part_of * chunk, chunk, HEAD_DIM)

                def dispatch(i, carry):
                    place, e = expert_at(i, side)
                    send(
                        sbuf.at[at(e * slots, slots, slots), there],
                        xbuf.at[at(place * slots, slots, slots), theirs],
                        disp_send,
                        disp_sem.at[part_of, side],
                        {"expert": e},
                    )
                    return carry

                lax.fori_loop(0, GROUP * half_planes - side, dispatch, 0)
                if side == 1:
                    local(
                        sbuf.at[at(me * slots, slots, slots), there],
                        xbuf.at[pl.ds((planes - 1) * slots, slots), theirs],
                        disp_sem.at[part_of, side],
                    )
        if not last:
            pump(1)

    pump(len(pending) - hops)

    gain = jnp.concatenate(
        [
            gainbuf[:, pl.ds((h * GROUP + peer) * HEAD_DIM, HEAD_DIM)]
            for peer in range(GROUP)
            for h in range(heads)
        ],
        axis=1,
    )
    hidden = wgf.shape[1]
    strip = min(256, hidden)
    part_rows = half_planes * slots

    def receive(side):
        for c in range(cols // chunk):
            wait(rbuf.at[pl.ds(0, experts // 2 * slots), pl.ds(c * chunk, chunk)], disp_sem.at[c, side])

        def normalise(g, carry):
            there = at(g * slots, slots, slots)
            row = xbuf[there, :].astype(F32)
            inverse = lax.rsqrt(jnp.sum(row * row, axis=-1, keepdims=True) * (1.0 / width) + 1e-05)
            xbuf[there, :] = (row * inverse * gain).astype(BF)
            return carry

        lax.fori_loop(side * half_planes, (side + 1) * half_planes, normalise, 0)

    def enter(side):
        mine = pl.ds(side * part_rows, part_rows)

        def inner(n, carry):
            there = at(n * strip, strip, strip)
            gate = jnp.dot(xbuf[mine, :], wgf[:, there], preferred_element_type=F32)
            upward = jnp.dot(xbuf[mine, :], wuf[:, there], preferred_element_type=F32)
            hbuf[mine, there] = (gate / (1.0 + jnp.exp(-gate)) * upward).astype(BF)
            return carry

        strips = hidden // strip
        lax.fori_loop(0, strips - strips // 2, inner, 0)
        pump(1)
        lax.fori_loop(strips - strips // 2, strips, inner, 0)

    split = max(heads // 2, 1)
    returns = [(0, split)] + [(h, 1) for h in range(split, heads)]

    def leave(side, c):
        first_head, count = returns[c]
        start, size = first_head * HEAD_DIM, count * HEAD_DIM
        mine = pl.ds(side * part_rows, part_rows)
        landing = rbuf.at[at(me * slots, slots, slots), pl.ds(start, size)]
        for h in range(first_head, first_head + count):
            block = wdf[:, pl.ds(h * GROUP * HEAD_DIM, GROUP * HEAD_DIM)]
            result = jnp.dot(hbuf[mine, :], block, preferred_element_type=F32).astype(BF)
            for peer in range(GROUP):
                ybuf[mine, pl.ds(peer * cols + h * HEAD_DIM, HEAD_DIM)] = result[:, peer * HEAD_DIM : (peer + 1) * HEAD_DIM]

        def outer(j, carry):
            peer = mate(1 + j)
            theirs = at(peer * cols + start, size, HEAD_DIM)

            def give(i, inner_carry):
                place = side * half_planes + i
                plane = lax.rem(z + planes - offset_of(place), planes)
                e = plane * GROUP + peer
                source = ybuf.at[at(place * slots, slots, slots), theirs]

                @pl.when(e != me)
                def _():
                    send(source, landing, ret_send, ret_sem.at[c], {"expert": e})

                @pl.when(e == me)
                def _():
                    local(source, landing, ret_sem.at[c])

                return inner_carry

            lax.fori_loop(0, half_planes, give, 0)
            return carry

        lax.fori_loop(0, GROUP, outer, 0)

    receive(0)
    for piece in range(2):
        wait(weights[piece][0], own_sem.at[piece])
        wait(weights[piece][1].at[pl.ds(0, width // 2)], part_sem.at[piece])
    enter(0)
    for piece in (2, 3):
        wait(weights[piece][0], own_sem.at[piece])
    wait(wdf.at[pl.ds(0, hidden // 2), left], part_sem.at[2])
    leave(0, 0)
    pump(1)
    receive(1)
    enter(1)
    leave(1, 0)
    pump(len(pending))
    wait(wdf.at[pl.ds(0, hidden // 2), right], part_sem.at[3])
    for c in range(1, len(returns)):
        for side in range(2):
            leave(side, c)

    for c, (first_head, count) in enumerate(returns):
        here = pl.ds(first_head * HEAD_DIM, count * HEAD_DIM)
        finished = [(h, pl.ds(h * HEAD_DIM, HEAD_DIM)) for h in range(first_head, first_head + count)]
        wait(rbuf.at[:, here], ret_sem.at[c])

        def hand_over(peer):
            for h, lanes in finished:
                source = fbuf.at[at(peer * rows, rows, rows), lanes]
                send(source, out.at[:, head_at(x, h)], fin_send, fin_sem, in_group(peer))

        ready = None
        for i in (GROUP // 2, *(n for n in range(1, GROUP) if n != GROUP // 2), 0):
            there = at(mate(i) * rows, rows, rows)
            total = att[there, here].astype(F32) + jnp.dot(mix[there, :], rbuf[:, here], preferred_element_type=F32)
            fbuf[there, here] = total.astype(BF)
            if ready is not None:
                hand_over(ready)
            ready = mate(i)
        for h, lanes in finished:
            local(fbuf.at[own_rows, lanes], out.at[:, head_at(x, h)], fin_sem)

    for i in range(3):
        wait(qbuf.at[pl.ds(0, span - rows), :], qkv_send.at[i])
    for i in range(4):
        size = weights[i][0].shape[0]
        wait(weights[i][1].at[pl.ds(0, (dp - 1) * size)], w_send.at[i])
    wait(kbuf, halo_send)
    wait(metabuf.at[pl.ds(0, GROUP - 1)], meta_send)
    wait(metabuf.at[pl.ds(0, GROUP)], next_send)
    wait(rbuf.at[pl.ds(0, (experts - 1) * slots), :], disp_send)
    wait(rbuf.at[pl.ds(0, (experts - 1) * slots), :], ret_send)
    wait(qbuf.at[pl.ds(0, span - rows), :], fin_send)
    wait(out, fin_sem)


def per_device(
    experts,
    dp,
    queries,
    keys,
    values,
    doc_ids,
    expert_index,
    gates,
    capacity,
    norm_gain,
    gate_weight,
    up_weight,
    down_weight,
):
    rows, width = queries.shape[1:]
    hidden = gate_weight.shape[2]
    cols = width // GROUP
    span = GROUP * rows
    slots = GROUP * MOST
    heads = cols // HEAD_DIM
    hbm = pl.BlockSpec(memory_space=pl.ANY)
    dma = pltpu.SemaphoreType.DMA
    out = pl.pallas_call(
        functools.partial(layer_kernel, experts, dp),
        out_shape=pltpu.VMEM((rows, width), BF),
        in_specs=[hbm] * 11,
        out_specs=pl.BlockSpec(memory_space=pltpu.VMEM),
        scratch_shapes=[
            pltpu.VMEM((TOP, rows), jnp.int32),
            pltpu.VMEM((TOP, rows), F32),
            pltpu.VMEM((1, rows), jnp.int32),
            pltpu.VMEM((1, experts), jnp.int32),
            pltpu.VMEM((1, width), F32),
            pltpu.VMEM((span, cols), BF),
            pltpu.VMEM((2 * span, cols), BF),
            pltpu.VMEM((2 * span, cols), BF),
            pltpu.VMEM((2 * GROUP, 8, rows), F32),
            pltpu.VMEM((8, span), F32),
            pltpu.VMEM((span, 8), F32),
            pltpu.VMEM((8, 2 * span), F32),
            pltpu.VMEM((experts * slots, span), BF),
            pltpu.VMEM((span, experts * slots), BF),
            pltpu.VMEM((span, cols), BF),
            pltpu.VMEM((experts * slots, cols), BF),
            pltpu.VMEM((experts // GROUP * slots, width), BF),
            pltpu.VMEM((experts // GROUP * slots, hidden), BF),
            pltpu.VMEM((experts // GROUP * slots, width), BF),
            pltpu.VMEM((experts * slots, cols), BF),
            pltpu.VMEM((span, cols), BF),
            pltpu.VMEM((width, hidden), BF),
            pltpu.VMEM((width, hidden), BF),
            pltpu.VMEM((hidden, width), BF),
            dma((5,)),
            dma((heads,)),
            dma((heads,)),
            dma((heads,)),
            dma,
            dma,
            dma((2, 2)),
            dma((4,)),
            dma,
            dma((2, dp // 4, 4)),
            dma((4,)),
            dma((4,)),
            dma((3,)),
            dma,
            dma,
            dma,
            dma,
            dma,
            dma,
            dma((4,)),
            pltpu.SemaphoreType.REGULAR((2,)),
        ],
        compiler_params=pltpu.CompilerParams(
            collective_id=0, has_side_effects=True, vmem_limit_bytes=56 * 1024 * 1024
        ),
        name="layer",
    )(
        queries[0],
        keys[0],
        values[0],
        expert_index[0].T,
        gates[0].T,
        doc_ids,
        capacity[None, :],
        norm_gain[None, :],
        gate_weight[0],
        up_weight[0],
        down_weight[0],
    )
    return out[None]


def solution(mesh):
    placed = (
        P("dp", "expert", None),
        P("dp", "expert", None),
        P("dp", "expert", None),
        P("dp", "expert"),
        P("dp", "expert", None),
        P("dp", "expert", None),
        P(),
        P(),
        P("expert", "dp", None),
        P("expert", "dp", None),
        P("expert", "dp", None),
    )
    body = functools.partial(per_device, mesh.shape["expert"], mesh.shape["dp"])
    return jax.shard_map(body, mesh=mesh, in_specs=placed, out_specs=P("dp", "expert", None), check_vma=False)
```
